32 devices in a mesh: scan: 8 (over y, x, core), track: 4 (over z).
Axes of the slice: x: 2, y: 2, z: 4, core: 2. Of those that a mesh axis runs over, the one named last changes fastest.
Arguments:
- temp_before: float32 [2, 128, 128, 256], P(None, 'scan', 'track'), may hold values from -4 to 4
- temp_after: float32 [2, 128, 128, 256], P(None, 'scan', 'track'), may hold values from -4 to 4
- melt_phase: int32 [2, 128, 128, 256], P(None, 'scan', 'track'), may hold values from 0 to 2
- objective_grad: float32 [2, 128, 128, 256], P(None, 'scan', 'track'), may hold values from -6 to 6
- laser_path: int32 [2, 8], replicated, may hold values from 0 to 16383
Outputs:
- power_sensitivity: float32 [2, 128, 128, 256], P(None, 'scan', 'track')
- initial_adjoint: float32 [128, 128, 256], P('scan', 'track')
The draws below stay inside these ranges and needn't reach their ends.
Inputs may be any that keep to these rules, and one draw needn't show every extreme that they name: `laser_path`: each entry is a top-surface cell x * 128 + y of the window.
All inputs are finite; a program needn't handle non-finite values.
Results may differ from the reference program's by a relative error of at most 0.0001.
Values sent between devices are 32-bit elements; how exact they have to be, the bound alone decides.
A program may use at most 64 MiB of HBM per device.

```python
import jax
import jax.numpy as jnp
from jax import lax

CX = 16
CZ = 256
STEPS = 2
ITERS = 4
SPOTS = 8
NX = 128
NY = 128


def place_ends(entries, rng, low, high):
    place = [jax.random.randint(jax.random.fold_in(rng, axis), (), 0, length) for axis, length in enumerate(entries.shape)]
    widest = entries.shape.index(max(entries.shape))
    beside = place[:widest] + [(place[widest] + 1) % entries.shape[widest]] + place[widest + 1:]
    return entries.at[tuple(place)].set(low).at[tuple(beside)].set(high)


def levels(key, extent, split, least, high):
    factor_of = 1.0
    for axis_at, shards_of in split:
        draws = jax.random.uniform(jax.random.fold_in(jax.random.fold_in(key, 6), axis_at), (shards_of,), jnp.float32, least / len(split), high / len(split))
        factor_of = factor_of * jnp.repeat(jnp.exp(draws), extent[axis_at] // shards_of).reshape((-1,) + (1,) * (len(extent) - 1 - axis_at))
    return factor_of


def centred(stream_key, shape, scale, bound, shards=(), held_as=jnp.bfloat16):
    entries = jax.random.normal(stream_key, shape, jnp.float32) * scale
    if len(shards) > 0:
        entries = levels(stream_key, shape, shards, -0.22, 0.18) * entries
    return jnp.clip(entries, min=-bound, max=bound).astype(held_as)


def setup_inputs(seed: int = 0) -> dict:
    key_list = jax.random.split(jax.random.key(seed), 6)
    return {
        "temp_before": centred(key_list[0], (STEPS, NX, NY, CZ), 1.0, 4.0, ((1, 8), (2, 4)), jnp.float32),
        "temp_after": centred(key_list[1], (STEPS, NX, NY, CZ), 1.0, 4.0, ((1, 8), (2, 4)), jnp.float32),
        "melt_phase": place_ends(jax.random.randint(key_list[2], (STEPS, NX, NY, CZ), 0, 3), jax.random.fold_in(key_list[2], 1), 0, 2).astype(jnp.int32),
        "objective_grad": centred(key_list[3], (STEPS, NX, NY, CZ), 1.0, 6.0, ((1, 8), (2, 4)), jnp.float32),
        "laser_path": place_ends(jax.random.randint(key_list[4], (STEPS, SPOTS), 0, NX * NY), jax.random.fold_in(key_list[4], 1), 0, (NX * NY) - 1).astype(jnp.int32),
    }


CAPS = (0.6, 2.0, 0.9)
ABSORBS = (0.35, 0.5, 0.65)
spot_radius = 3.0
decay_depth = 4.0
spot_peak = 4.0


def lookup(melt, values):
    return jnp.where(melt == 0, jnp.float32(values[0]), jnp.where(melt == 1, jnp.float32(values[1]), jnp.float32(values[2])))


def capacity_terms(before, melt):
    base = lookup(melt, CAPS)
    slope_tanh = jnp.tanh(before)
    return base * (1.0 + 0.5 * slope_tanh), base * 0.5 * (1.0 - slope_tanh * slope_tanh)


def source_field(path_row, x_start, y_start, rows_x, rows_y, rows_z, width_y):
    spot_x = (path_row // width_y).astype(jnp.float32)
    spot_y = (path_row % width_y).astype(jnp.float32)
    cells_x = (x_start + jnp.arange(rows_x, dtype=jnp.int32)).astype(jnp.float32)
    cells_y = (y_start + jnp.arange(rows_y, dtype=jnp.int32)).astype(jnp.float32)
    diff_x = cells_x[:, None] - spot_x[None, :]
    diff_y = cells_y[:, None] - spot_y[None, :]
    along_x = jnp.exp(-diff_x * diff_x / (2.0 * spot_radius * spot_radius))
    along_y = jnp.exp(-diff_y * diff_y / (2.0 * spot_radius * spot_radius))
    surface = jnp.dot(along_x, along_y.T, precision=lax.Precision.HIGHEST)
    depth_fall = spot_peak * jnp.exp(-jnp.arange(rows_z, dtype=jnp.float32) / decay_depth)
    return surface[:, :, None] * depth_fall[None, None, :]


def operate(vector, capacity):
    padded = jnp.pad(vector, 1)
    beside = padded[2:, 1:-1, 1:-1] + padded[:-2, 1:-1, 1:-1]
    beside = beside + padded[1:-1, 2:, 1:-1] + padded[1:-1, :-2, 1:-1]
    beside = beside + padded[1:-1, 1:-1, 2:] + padded[1:-1, 1:-1, :-2]
    return (6.0 + capacity) * vector - beside


def solve(source_side, capacity):
    solution = jnp.zeros_like(source_side)
    residual = source_side
    direction = source_side
    norm_now = jnp.sum(residual * residual)
    for iteration in range(ITERS):
        applied = operate(direction, capacity)
        step_length = norm_now / jnp.sum(direction * applied)
        solution = solution + step_length * direction
        residual = residual - step_length * applied
        norm_next = jnp.sum(residual * residual)
        direction = residual + (norm_next / norm_now) * direction
        norm_now = norm_next
    return solution


def reference(temp_before, temp_after, melt_phase, objective_grad, laser_path):
    carry = jnp.zeros((NX, NY, CZ), jnp.float32)
    results = [None] * STEPS
    for section in reversed(range(STEPS)):
        capacity, capacity_slope = capacity_terms(temp_before[section], melt_phase[section])
        moved = jnp.concatenate([jnp.zeros((CX, NY, CZ), jnp.float32), carry[:-CX]], 0)
        source_side = objective_grad[section] + moved
        adjoint = solve(source_side, capacity)
        weight = lookup(melt_phase[section], ABSORBS) * (1.0 + source_field(laser_path[section], 0, 0, NX, NY, CZ, NY))
        results[section] = weight * adjoint
        carry = (capacity - capacity_slope * (temp_after[section] - temp_before[section])) * adjoint
    return jnp.stack(results, 0), carry
```

```python
import functools

import jax
import jax.numpy as jnp
from jax import lax
from jax.experimental import pallas as pl
from jax.experimental.pallas import tpu as pltpu
from jax.sharding import PartitionSpec as P

ITERS = 4
CAPS = (0.6, 2.0, 0.9)
ABSORBS = (0.35, 0.5, 0.65)
spot_radius = 3.0
decay_depth = 4.0
spot_peak = 4.0

SHIFT = 7.25
SCALE = 3.0

HX = 4
HY = 8

DIRS = tuple((dx, dy) for dx in (-1, 0, 1) for dy in (-1, 0, 1) if (dx, dy) != (0, 0))
PAIRS = tuple((i, j) for i in range(ITERS) for j in range(i, ITERS)) + ((ITERS - 1, ITERS),)
MESH = pl.DeviceIdType.MESH
LANES = 128
CHUNKS = 4
TRIPS = 2


def lookup(melt, values):
    return jnp.where(
        melt == 0,
        jnp.float32(values[0]),
        jnp.where(melt == 1, jnp.float32(values[1]), jnp.float32(values[2])),
    )


def solve_small(g):
    def gram(i, j):
        return g[(min(i, j), max(i, j))]

    n = ITERS
    h = {}
    for i in range(n):
        for j in range(i, n):
            value = SCALE * gram(i + 1, j) + SHIFT * gram(i, j)
            if i > 0:
                value = value + SCALE * gram(i - 1, j)
            h[(i, j)] = value
    low, inv, y = {}, {}, {}
    for j in range(n):
        d = h[(j, j)]
        for k in range(j):
            d = d - low[(j, k)] * low[(j, k)] * inv[("d", k)]
        good = d > 1e-7 * h[(j, j)]
        inv[("d", j)] = jnp.where(good, d, 0.0)
        inv[j] = jnp.where(good, 1.0 / jnp.where(good, d, 1.0), 0.0)
        for i in range(j + 1, n):
            t = h[(j, i)]
            for k in range(j):
                t = t - low[(i, k)] * low[(j, k)] * inv[("d", k)]
            low[(i, j)] = t * inv[j]
    for i in range(n):
        t = gram(0, i)
        for k in range(i):
            t = t - low[(i, k)] * y[k]
        y[i] = t
    a = [None] * n
    for i in reversed(range(n)):
        t = y[i] * inv[i]
        for k in range(i + 1, n):
            t = t - low[(k, i)] * a[k]
        a[i] = t
    return a


def kernel(n, m, tb_in, ta_in, melt_in, grad_in, path, out_ps, out_carry,
           tb, ta, melt, grad, e1, ec0, er0, v, fac, wgt, cs, cr, part, red,
           load_sem, h_send, h_recv, c_send, c_recv, r_send, r_recv, known):
    rx, ry, rz = tb.shape[1:]
    ex, ey = rx + 2 * HX, ry + 2 * HY
    nz = rz // LANES
    d = lax.axis_index("scan")
    t = lax.axis_index("track")

    def exists(dx, dy):
        ok = None
        if dx < 0:
            ok = d > 0
        if dx > 0:
            ok = d < n - 1
        if dy != 0:
            oky = (t > 0) if dy < 0 else (t < m - 1)
            ok = oky if ok is None else jnp.logical_and(ok, oky)
        return ok

    def at_distance(r):
        for dx, dy in DIRS:
            ok = None
            if dx != 0:
                ok = (d >= r) if dx < 0 else (d < n - r)
            if dy != 0:
                oky = (t >= r) if dy < 0 else (t < m - r)
                ok = oky if ok is None else jnp.logical_and(ok, oky)
            if (dx == 0 or r < n) and (dy == 0 or r < m):
                yield ok, (d + dx * r, t + dy * r)

    def greet(sem, r):
        for ok, device in at_distance(r):
            @pl.when(ok)
            def _(device=device):
                pl.semaphore_signal(sem, inc=1, device_id=device, device_id_type=MESH)

    def greeted(sem, r):
        count = jnp.int32(0)
        for ok, _ in at_distance(r):
            count = count + ok.astype(jnp.int32)
        pl.semaphore_wait(sem, count)

    barrier = pltpu.get_barrier_semaphore()
    greet(barrier, 1)

    def zero_halo(ref):
        @pl.when(d == 0)
        def _():
            ref[0:HX] = jnp.zeros((HX, nz, ey, LANES), jnp.float32)

        @pl.when(d == n - 1)
        def _():
            ref[ex - HX:ex] = jnp.zeros((HX, nz, ey, LANES), jnp.float32)

        @pl.when(t == 0)
        def _():
            ref[:, :, 0:HY] = jnp.zeros((ex, nz, HY, LANES), jnp.float32)

        @pl.when(t == m - 1)
        def _():
            ref[:, :, ey - HY:ey] = jnp.zeros((ex, nz, HY, LANES), jnp.float32)

    def zs(z):
        return slice(z * LANES, (z + 1) * LANES)

    loads = []
    for q, (s, kind) in enumerate([(1, 2), (1, 0), (1, 1), (1, 3), (0, 0), (0, 1), (0, 2), (0, 3)]):
        if (s, kind) == (1, 2):
            parts = [
                pltpu.make_async_copy(
                    grad_in.at[1, :, :, pl.ds(z * LANES, LANES)],
                    e1.at[0, pl.ds(HX, rx), z, pl.ds(HY, ry)],
                    load_sem.at[8 + z],
                )
                for z in range(nz)
            ]
        else:
            src, dst = ((tb_in, tb), (melt_in, melt), (grad_in, grad), (ta_in, ta))[kind]
            where = 0 if kind == 2 else s
            parts = [pltpu.make_async_copy(src.at[s], dst.at[where], load_sem.at[q])]
        loads.append(parts)

    def loaded(*which):
        for q in which:
            for c in loads[q]:
                c.wait()

    for parts in loads:
        for c in parts:
            c.start()
    zero_halo(e1.at[0])
    zero_halo(er0)

    @pl.when(d == 0)
    def _():
        cr[...] = jnp.zeros(cr.shape, jnp.float32)


    def terms(s, x):
        base = lookup(melt[s, x], CAPS)
        h = jnp.tanh(tb[s, x])
        return base * (1.0 + 0.5 * h), base, h

    def diagonals(s, cap_ref):
        def body(x, _):
            cap, _, _ = terms(s, x)
            cap = (cap + (6.0 - SHIFT)) * (1.0 / SCALE)
            for z in range(nz):
                cap_ref[x + HX, z, HY:HY + ry] = cap[:, zs(z)]
            return 0

        lax.fori_loop(0, rx, body, 0)

    def factors(s):
        def body(x, _):
            cap, base, h = terms(s, x)
            slope = base * 0.5 * (1.0 - h * h)
            fac[s, x] = cap - slope * (ta[s, x] - tb[s, x])
            return 0

        lax.fori_loop(0, rx, body, 0)

    waves = known.shape[0]

    def spread(step):
        if 0 < step <= waves:
            greeted(known.at[step - 1], 2 ** (step - 1))
        if step < waves:
            greet(known.at[step], 2 ** step)
        return step + 1

    loaded(0)
    greeted(barrier, 1)

    XS = {-1: (slice(HX, 2 * HX), slice(ex - HX, ex)),
          0: (slice(HX, HX + rx), slice(HX, HX + rx)),
          1: (slice(rx, rx + HX), slice(0, HX))}
    YS = {-1: (slice(HY, HY + HX), slice(ey - HY, ey - HY + HX)),
          0: (slice(HY, HY + ry), slice(HY, HY + ry)),
          1: (slice(HY + ry - HX, HY + ry), slice(HY - HX, HY))}

    def halo_copy(ref, which, q):
        dx, dy = DIRS[q]
        x_src, x_dst = XS[dx]
        if which in (1, 3) and dx != 0:
            cut = (0, -1) if dx < 0 else (1, 0)
            x_src, x_dst = [slice(w.start + cut[0], w.stop + cut[1]) for w in (x_src, x_dst)]
        ds = lambda s: pl.ds(s.start, s.stop - s.start)
        return pltpu.make_async_remote_copy(
            src_ref=ref.at[ds(x_src), slice(None), ds(YS[dy][0])],
            dst_ref=ref.at[ds(x_dst), slice(None), ds(YS[dy][1])],
            send_sem=h_send.at[which, q],
            recv_sem=h_recv.at[which, q],
            device_id=(d + dx, t + dy),
            device_id_type=MESH,
        )

    def halo_start(ref, which, sides=(-1, 0, 1)):
        for q, (dx, dy) in enumerate(DIRS):
            if dx in sides:
                @pl.when(exists(dx, dy))
                def _(q=q):
                    halo_copy(ref, which, q).start()

    def halo_wait(ref, which):
        for q, (dx, dy) in enumerate(DIRS):
            @pl.when(exists(-dx, -dy))
            def _(q=q):
                halo_copy(ref, which, q).wait_recv()

    def halo_done(ref, which):
        for q, (dx, dy) in enumerate(DIRS):
            @pl.when(exists(dx, dy))
            def _(q=q):
                halo_copy(ref, which, q).wait_send()

    lane8 = lax.broadcasted_iota(jnp.int32, (8, LANES), 1)
    first, final = lane8 == 0, lane8 == LANES - 1

    def powers(v0, cap_ref):
        at = [v0] + [v.at[k] for k in range(ITERS)]
        for k in range(ITERS):
            tiles = range(HY, HY + ry, 8) if k == ITERS - 1 else range(HY - 4, HY + ry + 4, 8)

            planes = (ex - 2 * k - 2) // TRIPS

            def trip(p, _, k=k, tiles=tiles, planes=planes):
                x = k + 1 + planes * p
                for r in tiles:
                    c = [[at[k][x + q, z, r:r + 8] for z in range(nz)] for q in range(-1, planes + 1)]
                    for q in range(planes):
                        mid = c[q + 1]
                        up = [pltpu.roll(w, 1, 1) for w in mid]
                        down = [pltpu.roll(w, LANES - 1, 1) for w in mid]
                        for z in range(nz):
                            above = jnp.where(first, up[z - 1] if z > 0 else 0.0, up[z])
                            below = jnp.where(final, down[z + 1] if z < nz - 1 else 0.0, down[z])
                            beside = (c[q][z] + c[q + 2][z]) + (above + below)
                            beside = beside + (at[k][x + q, z, r - 1:r + 7] + at[k][x + q, z, r + 1:r + 9])
                            new = cap_ref[x + q, z, r:r + 8] * mid[z] - beside * (1.0 / SCALE)
                            if k > 0:
                                new = new - at[k - 1][x + q, z, r:r + 8]
                            at[k + 1][x + q, z, r:r + 8] = new
                return 0

            lax.fori_loop(0, TRIPS, trip, 0)
            if k < ITERS - 1:
                zero_halo(at[k + 1])

    def dots(v0, slot):
        at = [v0] + [v.at[k] for k in range(ITERS)]

        def body(x, acc):
            acc = list(acc)
            for z in range(nz):
                vals = [ref[x, z, HY:HY + ry] for ref in at]
                for q, (i, j) in enumerate(PAIRS):
                    acc[q] = acc[q] + (vals[i] * vals[j]).reshape(ry // 8, 8, LANES).sum(0)
            return tuple(acc)

        acc = lax.fori_loop(HX, HX + rx, body, tuple(jnp.zeros((8, LANES), jnp.float32) for _ in PAIRS))
        lane = lax.broadcasted_iota(jnp.int32, (1, LANES), 1)
        row = jnp.zeros((1, LANES), jnp.float32)
        for q, a in enumerate(acc):
            s = jnp.sum(jnp.sum(a, axis=0, keepdims=True), axis=1, keepdims=True)
            row = jnp.where(lane == q, s, row)
        part[slot, 0:1] = row

    me = d * m + t
    others = n * m - 1

    def sum_copy(slot, device):
        return pltpu.make_async_remote_copy(
            src_ref=part.at[slot, pl.ds(0, 1)],
            dst_ref=red.at[slot, pl.ds(me, 1)],
            send_sem=r_send.at[slot],
            recv_sem=r_recv.at[slot],
            device_id=device,
            device_id_type=MESH,
        )

    def sum_start(slot):
        for j in range(m):
            row = jnp.where(2 * t < m, m - 1 - j, j)
            for k in range(n):
                column = lax.rem(d + (n // 2 + k) % n, n)
                if (n // 2 + k) % n == 0:
                    @pl.when(row != t)
                    def _(row=row):
                        sum_copy(slot, (d, row)).start()
                else:
                    sum_copy(slot, (column, row)).start()
        red[slot, pl.ds(me, 1)] = part[slot, 0:1]

    def all_others(ref, sem):
        view = ref.at[pl.ds(0, others)]
        pltpu.make_async_copy(view, view, sem).wait()

    def sum_end(slot):
        all_others(red.at[slot], r_recv.at[slot])
        total = jnp.sum(red[slot], axis=0, keepdims=True)
        lane = lax.broadcasted_iota(jnp.int32, (1, LANES), 1)
        g = {}
        for q, pair in enumerate(PAIRS):
            g[pair] = jnp.sum(jnp.where(lane == q, total, 0.0), axis=1, keepdims=True)
        return solve_small(g)

    def sum_done(slot):
        all_others(red.at[slot], r_send.at[slot])

    def adjoint(v0, coef, x, z):
        out = coef[0] * v0[x + HX, z, HY:HY + ry]
        for k in range(1, ITERS):
            out = out + coef[k] * v[k - 1, x + HX, z, HY:HY + ry]
        return out

    def weights(s):
        width = m * ry
        yy = (t * ry + lax.broadcasted_iota(jnp.int32, (ry, 128), 0)).astype(jnp.float32)
        xx = (d * rx + lax.broadcasted_iota(jnp.int32, (ry, 128), 1)).astype(jnp.float32)
        two = 2.0 * spot_radius * spot_radius
        surface = jnp.zeros((ry, 128), jnp.float32)
        for k in range(path.shape[1]):
            cell = path[s, k]
            dx = xx - lax.div(cell, jnp.int32(width)).astype(jnp.float32)
            dy = yy - lax.rem(cell, jnp.int32(width)).astype(jnp.float32)
            surface = surface + jnp.exp(-dx * dx / two) * jnp.exp(-dy * dy / two)
        zz = lax.broadcasted_iota(jnp.int32, (1, rz), 1).astype(jnp.float32)
        fall = spot_peak * jnp.exp(-zz / decay_depth)
        lane = lax.broadcasted_iota(jnp.int32, (ry, 128), 1)

        def body(x, _):
            column = jnp.sum(jnp.where(lane == x, surface, 0.0), axis=1, keepdims=True)
            wgt[s, x] = lookup(melt[s, x], ABSORBS) * (1.0 + column * fall)
            return 0

        lax.fori_loop(0, rx, body, 0)

    halo_start(e1.at[0], 0)
    step = spread(0)
    loaded(1, 2)
    diagonals(1, e1.at[1])
    halo_start(e1.at[1], 3)
    step = spread(step)
    loaded(4, 5)
    diagonals(0, ec0)
    halo_start(ec0, 1)
    step = spread(step)
    loaded(3)
    factors(1)
    loaded(7)
    factors(0)
    while step < waves:
        step = spread(step)
    spread(step)
    halo_wait(e1.at[0], 0)
    halo_wait(e1.at[1], 3)
    powers(e1.at[0], e1.at[1])
    dots(e1.at[0], 0)
    sum_start(0)
    weights(1)
    weights(0)
    loaded(6)
    coef = sum_end(0)

    depth = rx // CHUNKS
    order = [CHUNKS - 1, 0] + list(range(1, CHUNKS - 1))

    def carry_body(x, _):
        for z in range(nz):
            cs[x, :, zs(z)] = fac[1, x, :, zs(z)] * adjoint(e1.at[0], coef, x, z)
        return 0

    def carry_copy(c):
        piece = pl.ds(c * depth, depth)
        return pltpu.make_async_remote_copy(
            src_ref=cs.at[piece], dst_ref=cr.at[piece], send_sem=c_send.at[c], recv_sem=c_recv.at[c],
            device_id=(d + 1, t), device_id_type=MESH)

    for c in order:
        lax.fori_loop(c * depth, (c + 1) * depth, carry_body, 0)

        @pl.when(d < n - 1)
        def _(c=c):
            carry_copy(c).start()

    def ps_late(x, _):
        for z in range(nz):
            out_ps[1, x, :, zs(z)] = wgt[1, x, :, zs(z)] * adjoint(e1.at[0], coef, x, z)
        return 0

    lax.fori_loop(0, rx, ps_late, 0)

    def rhs_body(x, _):
        for z in range(nz):
            er0[x + HX, z, HY:HY + ry] = grad[0, x, :, zs(z)] + cr[x, :, zs(z)]
        return 0

    for c in order:
        @pl.when(d > 0)
        def _(c=c):
            carry_copy(c).wait_recv()

        lax.fori_loop(c * depth, (c + 1) * depth, rhs_body, 0)
        if c == CHUNKS - 1:
            halo_start(er0, 2, (1,))
        if c == 0:
            halo_start(er0, 2, (-1,))
    halo_start(er0, 2, (0,))
    halo_wait(ec0, 1)
    halo_wait(er0, 2)
    powers(er0, ec0)
    dots(er0, 1)
    sum_start(1)
    coef0 = sum_end(1)

    def last(x, _):
        for z in range(nz):
            a = adjoint(er0, coef0, x, z)
            out_ps[0, x, :, zs(z)] = wgt[0, x, :, zs(z)] * a
            out_carry[x, :, zs(z)] = fac[0, x, :, zs(z)] * a
        return 0

    lax.fori_loop(0, rx, last, 0)
    halo_done(e1.at[0], 0)
    halo_done(e1.at[1], 3)
    halo_done(ec0, 1)
    halo_done(er0, 2)
    sum_done(0)
    sum_done(1)

    @pl.when(d < n - 1)
    def _():
        for c in order:
            carry_copy(c).wait_send()


def per_device(n, m, temp_before, temp_after, melt_phase, objective_grad, laser_path):
    steps, rx, ry, rz = temp_before.shape
    ex, ey = rx + 2 * HX, ry + 2 * HY
    nz = rz // LANES
    waves = (max(n, m) - 2).bit_length()
    f32 = jnp.float32
    vm = pl.BlockSpec(memory_space=pltpu.VMEM)
    dma = pltpu.SemaphoreType.DMA
    return pl.pallas_call(
        functools.partial(kernel, n, m),
        out_shape=(
            pltpu.VMEM((steps, rx, ry, rz), f32),
            pltpu.VMEM((rx, ry, rz), f32),
        ),
        in_specs=[pl.BlockSpec(memory_space=pl.ANY)] * 4 + [pl.BlockSpec(memory_space=pltpu.SMEM)],
        out_specs=(vm, vm),
        scratch_shapes=[
            pltpu.VMEM((2, rx, ry, rz), f32),
            pltpu.VMEM((2, rx, ry, rz), f32),
            pltpu.VMEM((2, rx, ry, rz), jnp.int32),
            pltpu.VMEM((1, rx, ry, rz), f32),
            pltpu.VMEM((2, ex, nz, ey, LANES), f32),
            pltpu.VMEM((ex, nz, ey, LANES), f32),
            pltpu.VMEM((ex, nz, ey, LANES), f32),
            pltpu.VMEM((ITERS, ex, nz, ey, LANES), f32),
            pltpu.VMEM((2, rx, ry, rz), f32),
            pltpu.VMEM((2, rx, ry, rz), f32),
            pltpu.VMEM((rx, ry, rz), f32),
            pltpu.VMEM((rx, ry, rz), f32),
            pltpu.VMEM((2, 8, LANES), f32),
            pltpu.VMEM((2, n * m, LANES), f32),
            dma((8 + nz,)),
            dma((4, 8)), dma((4, 8)),
            dma((CHUNKS,)), dma((CHUNKS,)),
            dma((2,)), dma((2,)),
            pltpu.SemaphoreType.REGULAR((waves,)),
        ],
        compiler_params=pltpu.CompilerParams(
            collective_id=0, has_side_effects=True, vmem_limit_bytes=60 * 1024 * 1024
        ),
    )(temp_before, temp_after, melt_phase, objective_grad, laser_path)


def solution(mesh):
    spec = P(None, "scan", "track", None)
    return jax.shard_map(
        functools.partial(per_device, mesh.shape["scan"], mesh.shape["track"]),
        mesh=mesh,
        in_specs=(spec, spec, spec, spec, P()),
        out_specs=(spec, P("scan", "track", None)),
        check_vma=False,
    )
```

```python
import functools

import jax
import jax.numpy as jnp
from jax import lax
from jax.experimental import pallas as pl
from jax.experimental.pallas import tpu as pltpu
from jax.sharding import PartitionSpec as P

ITERS = 4
CAPS = (0.6, 2.0, 0.9)
ABSORBS = (0.35, 0.5, 0.65)
spot_radius = 3.0
decay_depth = 4.0
spot_peak = 4.0

SHIFT = 7.25
SCALE = 3.0

HX = 4
HY = 8

DIRS = tuple((dx, dy) for dx in (-1, 0, 1) for dy in (-1, 0, 1) if (dx, dy) != (0, 0))
PAIRS = tuple((i, j) for i in range(ITERS) for j in range(i, ITERS)) + ((ITERS - 1, ITERS),)
MESH = pl.DeviceIdType.MESH
LANES = 128
CHUNKS = 4
TRIPS = 2
DOT_TRIPS = 4


def lookup(melt, values):
    return jnp.where(
        melt == 0,
        jnp.float32(values[0]),
        jnp.where(melt == 1, jnp.float32(values[1]), jnp.float32(values[2])),
    )


def solve_small(g):
    def gram(i, j):
        return g[(min(i, j), max(i, j))]

    n = ITERS
    h = {}
    for i in range(n):
        for j in range(i, n):
            value = SCALE * gram(i + 1, j) + SHIFT * gram(i, j)
            if i > 0:
                value = value + SCALE * gram(i - 1, j)
            h[(i, j)] = value
    low, inv, y = {}, {}, {}
    for j in range(n):
        d = h[(j, j)]
        for k in range(j):
            d = d - low[(j, k)] * low[(j, k)] * inv[("d", k)]
        good = d > 1e-7 * h[(j, j)]
        inv[("d", j)] = jnp.where(good, d, 0.0)
        inv[j] = jnp.where(good, 1.0 / jnp.where(good, d, 1.0), 0.0)
        for i in range(j + 1, n):
            t = h[(j, i)]
            for k in range(j):
                t = t - low[(i, k)] * low[(j, k)] * inv[("d", k)]
            low[(i, j)] = t * inv[j]
    for i in range(n):
        t = gram(0, i)
        for k in range(i):
            t = t - low[(i, k)] * y[k]
        y[i] = t
    a = [None] * n
    for i in reversed(range(n)):
        t = y[i] * inv[i]
        for k in range(i + 1, n):
            t = t - low[(k, i)] * a[k]
        a[i] = t
    return a


def kernel(n, m, tb_in, ta_in, melt_in, grad_in, path, out_ps, out_carry,
           tb, ta, melt, grad, e1, ec0, er0, v, fac, wgt, cs, cr, part, red,
           load_sem, h_send, h_recv, c_send, c_recv, r_send, r_recv, known):
    rx, ry, rz = tb.shape[1:]
    ex, ey = rx + 2 * HX, ry + 2 * HY
    nz = rz // LANES
    d = lax.axis_index("scan")
    t = lax.axis_index("track")

    def exists(dx, dy):
        ok = None
        if dx < 0:
            ok = d > 0
        if dx > 0:
            ok = d < n - 1
        if dy != 0:
            oky = (t > 0) if dy < 0 else (t < m - 1)
            ok = oky if ok is None else jnp.logical_and(ok, oky)
        return ok

    def at_distance(r):
        for dx, dy in DIRS:
            ok = None
            if dx != 0:
                ok = (d >= r) if dx < 0 else (d < n - r)
            if dy != 0:
                oky = (t >= r) if dy < 0 else (t < m - r)
                ok = oky if ok is None else jnp.logical_and(ok, oky)
            if (dx == 0 or r < n) and (dy == 0 or r < m):
                yield ok, (d + dx * r, t + dy * r)

    def greet(sem, r):
        for ok, device in at_distance(r):
            @pl.when(ok)
            def _(device=device):
                pl.semaphore_signal(sem, inc=1, device_id=device, device_id_type=MESH)

    def greeted(sem, r):
        count = jnp.int32(0)
        for ok, _ in at_distance(r):
            count = count + ok.astype(jnp.int32)
        pl.semaphore_wait(sem, count)

    barrier = pltpu.get_barrier_semaphore()
    greet(barrier, 1)

    def zero_halo(ref):
        @pl.when(d == 0)
        def _():
            ref[0:HX] = jnp.zeros((HX, nz, ey, LANES), jnp.float32)

        @pl.when(d == n - 1)
        def _():
            ref[ex - HX:ex] = jnp.zeros((HX, nz, ey, LANES), jnp.float32)

        @pl.when(t == 0)
        def _():
            ref[:, :, 0:HY] = jnp.zeros((ex, nz, HY, LANES), jnp.float32)

        @pl.when(t == m - 1)
        def _():
            ref[:, :, ey - HY:ey] = jnp.zeros((ex, nz, HY, LANES), jnp.float32)

    def zs(z):
        return slice(z * LANES, (z + 1) * LANES)

    loads = []
    for q, (s, kind) in enumerate([(1, 2), (1, 0), (1, 1), (1, 3), (0, 0), (0, 1), (0, 2), (0, 3)]):
        if (s, kind) == (1, 2):
            parts = [
                pltpu.make_async_copy(
                    grad_in.at[1, :, :, pl.ds(z * LANES, LANES)],
                    e1.at[0, pl.ds(HX, rx), z, pl.ds(HY, ry)],
                    load_sem.at[8 + z],
                )
                for z in range(nz)
            ]
        else:
            src, dst = ((tb_in, tb), (melt_in, melt), (grad_in, grad), (ta_in, ta))[kind]
            where = 0 if kind == 2 else s
            parts = [pltpu.make_async_copy(src.at[s], dst.at[where], load_sem.at[q])]
        loads.append(parts)

    def loaded(*which):
        for q in which:
            for c in loads[q]:
                c.wait()

    for parts in loads:
        for c in parts:
            c.start()
    zero_halo(e1.at[0])
    zero_halo(er0)

    @pl.when(d == 0)
    def _():
        cr[...] = jnp.zeros(cr.shape, jnp.float32)


    def terms(s, x):
        base = lookup(melt[s, x], CAPS)
        h = jnp.tanh(tb[s, x])
        return base * (1.0 + 0.5 * h), base, h

    def diagonals(s, cap_ref):
        def body(x, _):
            cap, _, _ = terms(s, x)
            cap = (cap + (6.0 - SHIFT)) * (1.0 / SCALE)
            for z in range(nz):
                cap_ref[x + HX, z, HY:HY + ry] = cap[:, zs(z)]
            return 0

        lax.fori_loop(0, rx, body, 0)

    def factors(s):
        def body(x, _):
            cap, base, h = terms(s, x)
            slope = base * 0.5 * (1.0 - h * h)
            fac[s, x] = cap - slope * (ta[s, x] - tb[s, x])
            return 0

        lax.fori_loop(0, rx, body, 0)

    waves = known.shape[0]

    def spread(step):
        if 0 < step <= waves:
            greeted(known.at[step - 1], 2 ** (step - 1))
        if step < waves:
            greet(known.at[step], 2 ** step)
        return step + 1

    loaded(0)
    greeted(barrier, 1)

    def span(delta, low, count, width):
        if delta == 0:
            return low, low, count
        if delta > 0:
            return low + count - width, low - width, width
        return low, low + count, width

    def halo_copy(ref, which, q):
        dx, dy = DIRS[q]
        wide = ITERS if which in (0, 2) else ITERS - 1
        if dx != 0 and dy != 0:
            wx = wy = wide - 2 if dx > 0 and dy > 0 else wide - 1
        else:
            wx = wide - 1 if dx > 0 else wide
            wy = wide - 1 if dy > 0 else wide
        x_src, x_dst, x_size = span(dx, HX, rx, wx)
        y_src, y_dst, y_size = span(dy, HY, ry, wy)
        return pltpu.make_async_remote_copy(
            src_ref=ref.at[pl.ds(x_src, x_size), slice(None), pl.ds(y_src, y_size)],
            dst_ref=ref.at[pl.ds(x_dst, x_size), slice(None), pl.ds(y_dst, y_size)],
            send_sem=h_send.at[which, q],
            recv_sem=h_recv.at[which, q],
            device_id=(d + dx, t + dy),
            device_id_type=MESH,
        )

    def halo_start(ref, which, sides=(-1, 0, 1)):
        for q, (dx, dy) in enumerate(DIRS):
            if dx in sides:
                @pl.when(exists(dx, dy))
                def _(q=q):
                    halo_copy(ref, which, q).start()

    def halo_wait(ref, which):
        for q, (dx, dy) in enumerate(DIRS):
            @pl.when(exists(-dx, -dy))
            def _(q=q):
                halo_copy(ref, which, q).wait_recv()

    def halo_done(ref, which):
        for q, (dx, dy) in enumerate(DIRS):
            @pl.when(exists(dx, dy))
            def _(q=q):
                halo_copy(ref, which, q).wait_send()

    lane8 = lax.broadcasted_iota(jnp.int32, (8, LANES), 1)
    first, final = lane8 == 0, lane8 == LANES - 1

    def powers(v0, cap_ref):
        at = [v0] + [v.at[k] for k in range(ITERS - 1)]
        for k in range(ITERS - 1):
            tiles = range(HY - 4, HY + ry + 4, 8)
            start, count = HX - ITERS + 2 + k, rx + 2 * (ITERS - 2 - k) + 1
            trips = 3 if count % 3 == 0 else TRIPS
            if count % trips:
                start, count = start - 1, count + 1
            planes = count // trips

            def trip(p, _, k=k, tiles=tiles, planes=planes, start=start):
                x = start + planes * p
                for r in tiles:
                    c = [[at[k][x + q, z, r:r + 8] for z in range(nz)] for q in range(-1, planes + 1)]
                    for q in range(planes):
                        mid = c[q + 1]
                        up = [pltpu.roll(w, 1, 1) for w in mid]
                        down = [pltpu.roll(w, LANES - 1, 1) for w in mid]
                        for z in range(nz):
                            above = jnp.where(first, up[z - 1] if z > 0 else 0.0, up[z])
                            below = jnp.where(final, down[z + 1] if z < nz - 1 else 0.0, down[z])
                            beside = (c[q][z] + c[q + 2][z]) + (above + below)
                            beside = beside + (at[k][x + q, z, r - 1:r + 7] + at[k][x + q, z, r + 1:r + 9])
                            new = cap_ref[x + q, z, r:r + 8] * mid[z] - beside * (1.0 / SCALE)
                            if k > 0:
                                new = new - at[k - 1][x + q, z, r:r + 8]
                            at[k + 1][x + q, z, r:r + 8] = new
                return 0

            lax.fori_loop(0, trips, trip, 0)
            zero_halo(at[k + 1])

    def dots(v0, cap_ref, slot):
        at = [v0] + [v.at[k] for k in range(ITERS - 1)]
        group = max(1, rx // DOT_TRIPS)

        def body(p, acc):
            acc = list(acc)
            for g in range(group):
                x = HX + p * group + g
                for r in range(HY, HY + ry, 8):
                    tips = [at[-1][x, z, r:r + 8] for z in range(nz)]
                    for z in range(nz):
                        vals = [ref[x, z, r:r + 8] for ref in at[:-1]] + [tips[z]]
                        over = tips[z + 1] if z < nz - 1 else 0.0
                        below = pltpu.roll(jnp.where(first, over, tips[z]), LANES - 1, 1)
                        after = at[-1][x + 1, z, r:r + 8] + at[-1][x, z, r + 1:r + 9] + below
                        vals.append(cap_ref[x, z, r:r + 8] * tips[z] - after * (2.0 / SCALE))
                        for q, (i, j) in enumerate(PAIRS):
                            acc[q] = acc[q] + vals[i] * vals[j]
            return tuple(acc)

        acc = lax.fori_loop(0, rx // group, body, tuple(jnp.zeros((8, LANES), jnp.float32) for _ in PAIRS))
        lane = lax.broadcasted_iota(jnp.int32, (1, LANES), 1)
        row = jnp.zeros((1, LANES), jnp.float32)
        for q, a in enumerate(acc):
            s = jnp.sum(jnp.sum(a, axis=0, keepdims=True), axis=1, keepdims=True)
            row = jnp.where(lane == q, s, row)
        part[slot, 0:1] = row

    me = d * m + t
    others = n * m - 1

    def sum_copy(slot, device):
        return pltpu.make_async_remote_copy(
            src_ref=part.at[slot, pl.ds(0, 1)],
            dst_ref=red.at[slot, pl.ds(me, 1)],
            send_sem=r_send.at[slot],
            recv_sem=r_recv.at[slot],
            device_id=device,
            device_id_type=MESH,
        )

    def sum_start(slot):
        for j in range(m):
            row = jnp.where(2 * t < m, m - 1 - j, j)
            for k in range(n):
                column = lax.rem(d + (n // 2 + k) % n, n)
                if (n // 2 + k) % n == 0:
                    @pl.when(row != t)
                    def _(row=row):
                        sum_copy(slot, (d, row)).start()
                else:
                    sum_copy(slot, (column, row)).start()
        red[slot, pl.ds(me, 1)] = part[slot, 0:1]

    def all_others(ref, sem):
        view = ref.at[pl.ds(0, others)]
        pltpu.make_async_copy(view, view, sem).wait()

    def sum_end(slot):
        all_others(red.at[slot], r_recv.at[slot])
        total = jnp.sum(red[slot], axis=0, keepdims=True)
        lane = lax.broadcasted_iota(jnp.int32, (1, LANES), 1)
        g = {}
        for q, pair in enumerate(PAIRS):
            g[pair] = jnp.sum(jnp.where(lane == q, total, 0.0), axis=1, keepdims=True)
        g[PAIRS[-1]] = g[PAIRS[-1]] - g[(ITERS - 2, ITERS - 1)]
        return solve_small(g)

    def sum_done(slot):
        all_others(red.at[slot], r_send.at[slot])

    def adjoint(v0, coef, x, z):
        out = coef[0] * v0[x + HX, z, HY:HY + ry]
        for k in range(1, ITERS):
            out = out + coef[k] * v[k - 1, x + HX, z, HY:HY + ry]
        return out

    def weights(s):
        width = m * ry
        yy = (t * ry + lax.broadcasted_iota(jnp.int32, (ry, 128), 0)).astype(jnp.float32)
        xx = (d * rx + lax.broadcasted_iota(jnp.int32, (ry, 128), 1)).astype(jnp.float32)
        two = 2.0 * spot_radius * spot_radius
        surface = jnp.zeros((ry, 128), jnp.float32)
        for k in range(path.shape[1]):
            cell = path[s, k]
            dx = xx - lax.div(cell, jnp.int32(width)).astype(jnp.float32)
            dy = yy - lax.rem(cell, jnp.int32(width)).astype(jnp.float32)
            surface = surface + jnp.exp(-dx * dx / two) * jnp.exp(-dy * dy / two)
        zz = lax.broadcasted_iota(jnp.int32, (1, rz), 1).astype(jnp.float32)
        fall = spot_peak * jnp.exp(-zz / decay_depth)
        lane = lax.broadcasted_iota(jnp.int32, (ry, 128), 1)

        def body(x, _):
            column = jnp.sum(jnp.where(lane == x, surface, 0.0), axis=1, keepdims=True)
            wgt[s, x] = lookup(melt[s, x], ABSORBS) * (1.0 + column * fall)
            return 0

        lax.fori_loop(0, rx, body, 0)

    halo_start(e1.at[0], 0)
    step = spread(0)
    loaded(1, 2)
    diagonals(1, e1.at[1])
    halo_start(e1.at[1], 3)
    step = spread(step)
    loaded(4, 5)
    diagonals(0, ec0)
    halo_start(ec0, 1)
    step = spread(step)
    loaded(3)
    factors(1)
    loaded(7)
    factors(0)
    while step < waves:
        step = spread(step)
    spread(step)
    halo_wait(e1.at[0], 0)
    halo_wait(e1.at[1], 3)
    powers(e1.at[0], e1.at[1])
    dots(e1.at[0], e1.at[1], 0)
    sum_start(0)
    weights(1)
    weights(0)
    loaded(6)
    coef = sum_end(0)

    depth = rx // CHUNKS
    order = [CHUNKS - 1, 0] + list(range(1, CHUNKS - 1))

    def carry_body(x, _):
        for z in range(nz):
            cs[x, :, zs(z)] = fac[1, x, :, zs(z)] * adjoint(e1.at[0], coef, x, z)
        return 0

    def carry_copy(c):
        piece = pl.ds(c * depth, depth)
        return pltpu.make_async_remote_copy(
            src_ref=cs.at[piece], dst_ref=cr.at[piece], send_sem=c_send.at[c], recv_sem=c_recv.at[c],
            device_id=(d + 1, t), device_id_type=MESH)

    for c in order:
        lax.fori_loop(c * depth, (c + 1) * depth, carry_body, 0)

        @pl.when(d < n - 1)
        def _(c=c):
            carry_copy(c).start()

    def ps_late(x, _):
        for z in range(nz):
            out_ps[1, x, :, zs(z)] = wgt[1, x, :, zs(z)] * adjoint(e1.at[0], coef, x, z)
        return 0

    lax.fori_loop(0, rx, ps_late, 0)

    def rhs_body(x, _):
        for z in range(nz):
            er0[x + HX, z, HY:HY + ry] = grad[0, x, :, zs(z)] + cr[x, :, zs(z)]
        return 0

    for c in order:
        @pl.when(d > 0)
        def _(c=c):
            carry_copy(c).wait_recv()

        lax.fori_loop(c * depth, (c + 1) * depth, rhs_body, 0)
        if c == CHUNKS - 1:
            halo_start(er0, 2, (1,))
        if c == 0:
            halo_start(er0, 2, (-1,))
    halo_start(er0, 2, (0,))
    halo_wait(ec0, 1)
    halo_wait(er0, 2)
    powers(er0, ec0)
    dots(er0, ec0, 1)
    sum_start(1)
    coef0 = sum_end(1)

    def last(x, _):
        for z in range(nz):
            a = adjoint(er0, coef0, x, z)
            out_ps[0, x, :, zs(z)] = wgt[0, x, :, zs(z)] * a
            out_carry[x, :, zs(z)] = fac[0, x, :, zs(z)] * a
        return 0

    lax.fori_loop(0, rx, last, 0)
    halo_done(e1.at[0], 0)
    halo_done(e1.at[1], 3)
    halo_done(ec0, 1)
    halo_done(er0, 2)
    sum_done(0)
    sum_done(1)

    @pl.when(d < n - 1)
    def _():
        for c in order:
            carry_copy(c).wait_send()


def per_device(n, m, temp_before, temp_after, melt_phase, objective_grad, laser_path):
    steps, rx, ry, rz = temp_before.shape
    ex, ey = rx + 2 * HX, ry + 2 * HY
    nz = rz // LANES
    waves = (max(n, m) - 2).bit_length()
    f32 = jnp.float32
    vm = pl.BlockSpec(memory_space=pltpu.VMEM)
    dma = pltpu.SemaphoreType.DMA
    return pl.pallas_call(
        functools.partial(kernel, n, m),
        out_shape=(
            pltpu.VMEM((steps, rx, ry, rz), f32),
            pltpu.VMEM((rx, ry, rz), f32),
        ),
        in_specs=[pl.BlockSpec(memory_space=pl.ANY)] * 4 + [pl.BlockSpec(memory_space=pltpu.SMEM)],
        out_specs=(vm, vm),
        scratch_shapes=[
            pltpu.VMEM((2, rx, ry, rz), f32),
            pltpu.VMEM((2, rx, ry, rz), f32),
            pltpu.VMEM((2, rx, ry, rz), jnp.int32),
            pltpu.VMEM((1, rx, ry, rz), f32),
            pltpu.VMEM((2, ex, nz, ey, LANES), f32),
            pltpu.VMEM((ex, nz, ey, LANES), f32),
            pltpu.VMEM((ex, nz, ey, LANES), f32),
            pltpu.VMEM((ITERS - 1, ex, nz, ey, LANES), f32),
            pltpu.VMEM((2, rx, ry, rz), f32),
            pltpu.VMEM((2, rx, ry, rz), f32),
            pltpu.VMEM((rx, ry, rz), f32),
            pltpu.VMEM((rx, ry, rz), f32),
            pltpu.VMEM((2, 8, LANES), f32),
            pltpu.VMEM((2, n * m, LANES), f32),
            dma((8 + nz,)),
            dma((4, 8)), dma((4, 8)),
            dma((CHUNKS,)), dma((CHUNKS,)),
            dma((2,)), dma((2,)),
            pltpu.SemaphoreType.REGULAR((waves,)),
        ],
        compiler_params=pltpu.CompilerParams(
            collective_id=0, has_side_effects=True, vmem_limit_bytes=60 * 1024 * 1024
        ),
    )(temp_before, temp_after, melt_phase, objective_grad, laser_path)


def solution(mesh):
    spec = P(None, "scan", "track", None)
    return jax.shard_map(
        functools.partial(per_device, mesh.shape["scan"], mesh.shape["track"]),
        mesh=mesh,
        in_specs=(spec, spec, spec, spec, P()),
        out_specs=(spec, P("scan", "track", None)),
        check_vma=False,
    )
```

```python
import functools

import jax
import jax.numpy as jnp
from jax import lax
from jax.experimental import pallas as pl
from jax.experimental.pallas import tpu as pltpu
from jax.sharding import PartitionSpec as P

ITERS = 4
CAPS = (0.6, 2.0, 0.9)
ABSORBS = (0.35, 0.5, 0.65)
spot_radius = 3.0
decay_depth = 4.0
spot_peak = 4.0

SHIFT = 7.25
SCALE = 3.0

HX = 4
HY = 8

DIRS = tuple((dx, dy) for dx in (-1, 0, 1) for dy in (-1, 0, 1) if (dx, dy) != (0, 0))
BACK = ((-1, 0),)
AHEAD = ((1, -1), (1, 0), (1, 1))
ASIDE = ((0, -1), (0, 1))
PAIRS = tuple((i, j) for i in range(ITERS) for j in range(i, ITERS)) + ((ITERS - 1, ITERS),)
MESH = pl.DeviceIdType.MESH
LANES = 128
TRIPS = 2
DOT_TRIPS = 4


def lookup(melt, values):
    return jnp.where(
        melt == 0,
        jnp.float32(values[0]),
        jnp.where(melt == 1, jnp.float32(values[1]), jnp.float32(values[2])),
    )


def solve_small(g):
    def gram(i, j):
        return g[(min(i, j), max(i, j))]

    n = ITERS
    h = {}
    for i in range(n):
        for j in range(i, n):
            value = SCALE * gram(i + 1, j) + SHIFT * gram(i, j)
            if i > 0:
                value = value + SCALE * gram(i - 1, j)
            h[(i, j)] = value
    low, inv, y = {}, {}, {}
    for j in range(n):
        d = h[(j, j)]
        for k in range(j):
            d = d - low[(j, k)] * low[(j, k)] * inv[("d", k)]
        good = d > 1e-7 * h[(j, j)]
        inv[("d", j)] = jnp.where(good, d, 0.0)
        inv[j] = jnp.where(good, 1.0 / jnp.where(good, d, 1.0), 0.0)
        for i in range(j + 1, n):
            t = h[(j, i)]
            for k in range(j):
                t = t - low[(i, k)] * low[(j, k)] * inv[("d", k)]
            low[(i, j)] = t * inv[j]
    for i in range(n):
        t = gram(0, i)
        for k in range(i):
            t = t - low[(i, k)] * y[k]
        y[i] = t
    a = [None] * n
    for i in reversed(range(n)):
        t = y[i] * inv[i]
        for k in range(i + 1, n):
            t = t - low[(k, i)] * a[k]
        a[i] = t
    return a


def kernel(n, m, tb_in, ta_in, melt_in, grad_in, path, out_ps, out_carry,
           tb, ta, melt, e1, ec0, er0, v, fac, wgt, cs, cr, part, red,
           load_sem, h_send, h_recv, c_send, c_recv, r_send, r_recv, known):
    rx, ry, rz = tb.shape[1:]
    ex, ey = rx + 2 * HX, ry + 2 * HY
    nz = rz // LANES
    d = lax.axis_index("scan")
    t = lax.axis_index("track")

    def exists(dx, dy):
        ok = None
        if dx < 0:
            ok = d > 0
        if dx > 0:
            ok = d < n - 1
        if dy != 0:
            oky = (t > 0) if dy < 0 else (t < m - 1)
            ok = oky if ok is None else jnp.logical_and(ok, oky)
        return ok

    def at_distance(r):
        for dx, dy in DIRS:
            ok = None
            if dx != 0:
                ok = (d >= r) if dx < 0 else (d < n - r)
            if dy != 0:
                oky = (t >= r) if dy < 0 else (t < m - r)
                ok = oky if ok is None else jnp.logical_and(ok, oky)
            if (dx == 0 or r < n) and (dy == 0 or r < m):
                yield ok, (d + dx * r, t + dy * r)

    def greet(sem, r):
        for ok, device in at_distance(r):
            @pl.when(ok)
            def _(device=device):
                pl.semaphore_signal(sem, inc=1, device_id=device, device_id_type=MESH)

    def greeted(sem, r):
        count = jnp.int32(0)
        for ok, _ in at_distance(r):
            count = count + ok.astype(jnp.int32)
        pl.semaphore_wait(sem, count)

    barrier = pltpu.get_barrier_semaphore()
    greet(barrier, 1)

    def zero_halo(ref):
        @pl.when(d == 0)
        def _():
            ref[0:HX] = jnp.zeros((HX, nz, ey, LANES), jnp.float32)

        @pl.when(d == n - 1)
        def _():
            ref[ex - HX:ex] = jnp.zeros((HX, nz, ey, LANES), jnp.float32)

        @pl.when(t == 0)
        def _():
            ref[:, :, 0:HY] = jnp.zeros((ex, nz, HY, LANES), jnp.float32)

        @pl.when(t == m - 1)
        def _():
            ref[:, :, ey - HY:ey] = jnp.zeros((ex, nz, HY, LANES), jnp.float32)

    def zs(z):
        return slice(z * LANES, (z + 1) * LANES)

    loads = []
    for q, (s, kind) in enumerate([(1, 2), (1, 0), (1, 1), (1, 3), (0, 0), (0, 1), (0, 2), (0, 3)]):
        if kind == 2:
            where = e1.at[0] if s == 1 else er0
            parts = [
                pltpu.make_async_copy(
                    grad_in.at[s, :, :, pl.ds(z * LANES, LANES)],
                    where.at[pl.ds(HX, rx), z, pl.ds(HY, ry)],
                    load_sem.at[8 + s * nz + z],
                )
                for z in range(nz)
            ]
        else:
            src, dst = ((tb_in, tb), (melt_in, melt), None, (ta_in, ta))[kind]
            parts = [pltpu.make_async_copy(src.at[s], dst.at[s], load_sem.at[q])]
        loads.append(parts)

    def loaded(*which):
        for q in which:
            for c in loads[q]:
                c.wait()

    for parts in loads:
        for c in parts:
            c.start()
    zero_halo(e1.at[0])
    zero_halo(er0)

    def terms(s, x):
        base = lookup(melt[s, x], CAPS)
        h = jnp.tanh(tb[s, x])
        return base * (1.0 + 0.5 * h), base, h

    def diagonals(s, cap_ref):
        def body(x, _):
            cap, _, _ = terms(s, x)
            cap = (cap + (6.0 - SHIFT)) * (1.0 / SCALE)
            for z in range(nz):
                cap_ref[x + HX, z, HY:HY + ry] = cap[:, zs(z)]
            return 0

        lax.fori_loop(0, rx, body, 0)

    def factors(s):
        def body(x, _):
            cap, base, h = terms(s, x)
            slope = base * 0.5 * (1.0 - h * h)
            fac[s, x] = cap - slope * (ta[s, x] - tb[s, x])
            return 0

        lax.fori_loop(0, rx, body, 0)

    waves = known.shape[0]

    def spread(step):
        if 0 < step <= waves:
            greeted(known.at[step - 1], 2 ** (step - 1))
        if step < waves:
            greet(known.at[step], 2 ** step)
        return step + 1

    loaded(0)
    greeted(barrier, 1)

    def span(delta, low, count, width):
        if delta == 0:
            return low, low, count
        if delta > 0:
            return low + count - width, low - width, width
        return low, low + count, width

    def halo_copy(ref, which, q):
        dx, dy = DIRS[q]
        wide = ITERS if which in (0, 2) else ITERS - 1
        if dx != 0 and dy != 0:
            wx = wy = wide - 2 if dx > 0 and dy > 0 else wide - 1
        else:
            wx = wide - 1 if dx > 0 else wide
            wy = wide - 1 if dy > 0 else wide
        x_src, x_dst, x_size = span(dx, HX, rx, wx)
        y_src, y_dst, y_size = span(dy, HY, ry, wy)
        if which == 2 and dx == 0:
            x_size = rx + ITERS - 1
        return pltpu.make_async_remote_copy(
            src_ref=ref.at[pl.ds(x_src, x_size), slice(None), pl.ds(y_src, y_size)],
            dst_ref=ref.at[pl.ds(x_dst, x_size), slice(None), pl.ds(y_dst, y_size)],
            send_sem=h_send.at[which, q],
            recv_sem=h_recv.at[which, q],
            device_id=(d + dx, t + dy),
            device_id_type=MESH,
        )

    def halo_start(ref, which, wanted=DIRS):
        for q, (dx, dy) in enumerate(DIRS):
            if (dx, dy) in wanted:
                @pl.when(exists(dx, dy))
                def _(q=q):
                    halo_copy(ref, which, q).start()

    def halo_wait(ref, which, wanted=DIRS):
        for q, (dx, dy) in enumerate(DIRS):
            if (dx, dy) in wanted:
                @pl.when(exists(-dx, -dy))
                def _(q=q):
                    halo_copy(ref, which, q).wait_recv()

    def halo_done(ref, which, wanted=DIRS):
        for q, (dx, dy) in enumerate(DIRS):
            if (dx, dy) in wanted:
                @pl.when(exists(dx, dy))
                def _(q=q):
                    halo_copy(ref, which, q).wait_send()

    lane8 = lax.broadcasted_iota(jnp.int32, (8, LANES), 1)
    first, final = lane8 == 0, lane8 == LANES - 1

    def powers(v0, cap_ref):
        at = [v0] + [v.at[k] for k in range(ITERS - 1)]
        for k in range(ITERS - 1):
            tiles = range(HY - 4, HY + ry + 4, 8)
            start, count = HX - ITERS + 2 + k, rx + 2 * (ITERS - 2 - k) + 1
            trips = 3 if count % 3 == 0 else TRIPS
            if count % trips:
                start, count = start - 1, count + 1
            planes = count // trips

            def trip(p, _, k=k, tiles=tiles, planes=planes, start=start):
                x = start + planes * p
                for r in tiles:
                    c = [[at[k][x + q, z, r:r + 8] for z in range(nz)] for q in range(-1, planes + 1)]
                    for q in range(planes):
                        mid = c[q + 1]
                        up = [pltpu.roll(w, 1, 1) for w in mid]
                        down = [pltpu.roll(w, LANES - 1, 1) for w in mid]
                        for z in range(nz):
                            above = jnp.where(first, up[z - 1] if z > 0 else 0.0, up[z])
                            below = jnp.where(final, down[z + 1] if z < nz - 1 else 0.0, down[z])
                            beside = (c[q][z] + c[q + 2][z]) + (above + below)
                            beside = beside + (at[k][x + q, z, r - 1:r + 7] + at[k][x + q, z, r + 1:r + 9])
                            new = cap_ref[x + q, z, r:r + 8] * mid[z] - beside * (1.0 / SCALE)
                            if k > 0:
                                new = new - at[k - 1][x + q, z, r:r + 8]
                            at[k + 1][x + q, z, r:r + 8] = new
                return 0

            lax.fori_loop(0, trips, trip, 0)
            zero_halo(at[k + 1])

    def dots(v0, cap_ref, slot):
        at = [v0] + [v.at[k] for k in range(ITERS - 1)]
        group = max(1, rx // DOT_TRIPS)

        def body(p, acc):
            acc = list(acc)
            for g in range(group):
                x = HX + p * group + g
                for r in range(HY, HY + ry, 8):
                    tips = [at[-1][x, z, r:r + 8] for z in range(nz)]
                    for z in range(nz):
                        vals = [ref[x, z, r:r + 8] for ref in at[:-1]] + [tips[z]]
                        over = tips[z + 1] if z < nz - 1 else 0.0
                        below = pltpu.roll(jnp.where(first, over, tips[z]), LANES - 1, 1)
                        after = at[-1][x + 1, z, r:r + 8] + at[-1][x, z, r + 1:r + 9] + below
                        vals.append(cap_ref[x, z, r:r + 8] * tips[z] - after * (2.0 / SCALE))
                        for q, (i, j) in enumerate(PAIRS):
                            acc[q] = acc[q] + vals[i] * vals[j]
            return tuple(acc)

        acc = lax.fori_loop(0, rx // group, body, tuple(jnp.zeros((8, LANES), jnp.float32) for _ in PAIRS))
        lane = lax.broadcasted_iota(jnp.int32, (1, LANES), 1)
        row = jnp.zeros((1, LANES), jnp.float32)
        for q, a in enumerate(acc):
            s = jnp.sum(jnp.sum(a, axis=0, keepdims=True), axis=1, keepdims=True)
            row = jnp.where(lane == q, s, row)
        part[slot, 0:1] = row

    me = d * m + t
    others = n * m - 1

    def sum_copy(slot, device):
        return pltpu.make_async_remote_copy(
            src_ref=part.at[slot, pl.ds(0, 1)],
            dst_ref=red.at[slot, pl.ds(me, 1)],
            send_sem=r_send.at[slot],
            recv_sem=r_recv.at[slot],
            device_id=device,
            device_id_type=MESH,
        )

    def sum_start(slot):
        for j in range(m):
            row = jnp.where(2 * t < m, m - 1 - j, j)
            for k in range(n):
                column = lax.rem(d + (n // 2 + k) % n, n)
                if (n // 2 + k) % n == 0:
                    @pl.when(row != t)
                    def _(row=row):
                        sum_copy(slot, (d, row)).start()
                else:
                    sum_copy(slot, (column, row)).start()
        red[slot, pl.ds(me, 1)] = part[slot, 0:1]

    def all_others(ref, sem):
        view = ref.at[pl.ds(0, others)]
        pltpu.make_async_copy(view, view, sem).wait()

    def sum_end(slot):
        all_others(red.at[slot], r_recv.at[slot])
        total = jnp.sum(red[slot], axis=0, keepdims=True)
        lane = lax.broadcasted_iota(jnp.int32, (1, LANES), 1)
        g = {}
        for q, pair in enumerate(PAIRS):
            g[pair] = jnp.sum(jnp.where(lane == q, total, 0.0), axis=1, keepdims=True)
        g[PAIRS[-1]] = g[PAIRS[-1]] - g[(ITERS - 2, ITERS - 1)]
        return solve_small(g)

    def sum_done(slot):
        all_others(red.at[slot], r_send.at[slot])

    def adjoint(v0, coef, x, z, r=0, size=None):
        rows = slice(HY + r, HY + r + (size or ry))
        out = coef[0] * v0[x + HX, z, rows]
        for k in range(1, ITERS):
            out = out + coef[k] * v[k - 1, x + HX, z, rows]
        return out

    def weights(s):
        width = m * ry
        yy = (t * ry + lax.broadcasted_iota(jnp.int32, (ry, 128), 0)).astype(jnp.float32)
        xx = (d * rx + lax.broadcasted_iota(jnp.int32, (ry, 128), 1)).astype(jnp.float32)
        two = 2.0 * spot_radius * spot_radius
        surface = jnp.zeros((ry, 128), jnp.float32)
        for k in range(path.shape[1]):
            cell = path[s, k]
            dx = xx - lax.div(cell, jnp.int32(width)).astype(jnp.float32)
            dy = yy - lax.rem(cell, jnp.int32(width)).astype(jnp.float32)
            surface = surface + jnp.exp(-dx * dx / two) * jnp.exp(-dy * dy / two)
        zz = lax.broadcasted_iota(jnp.int32, (1, rz), 1).astype(jnp.float32)
        fall = spot_peak * jnp.exp(-zz / decay_depth)
        lane = lax.broadcasted_iota(jnp.int32, (ry, 128), 1)

        def body(x, _):
            column = jnp.sum(jnp.where(lane == x, surface, 0.0), axis=1, keepdims=True)
            wgt[s, x] = lookup(melt[s, x], ABSORBS) * (1.0 + column * fall)
            return 0

        lax.fori_loop(0, rx, body, 0)

    halo_start(e1.at[0], 0)
    step = spread(0)
    loaded(1, 2)
    diagonals(1, e1.at[1])
    halo_start(e1.at[1], 3)
    step = spread(step)
    loaded(4, 5)
    diagonals(0, ec0)
    halo_start(ec0, 1)
    step = spread(step)
    loaded(3)
    factors(1)
    loaded(7)
    factors(0)
    while step < waves:
        step = spread(step)
    spread(step)
    halo_wait(e1.at[0], 0)
    halo_wait(e1.at[1], 3)
    powers(e1.at[0], e1.at[1])
    dots(e1.at[0], e1.at[1], 0)
    sum_start(0)
    loaded(6)
    halo_start(er0, 2, BACK)
    weights(1)
    weights(0)
    coef = sum_end(0)

    tail = ITERS - 1
    body = rx - tail
    PIECES = ((body, tail, 0, ry), (0, body, 0, ITERS), (0, body, ry - tail, tail), (0, body, ITERS, ry - tail - ITERS))

    def carry_copy(c):
        x, xs, y, ys = PIECES[c]
        piece = (pl.ds(x, xs), slice(None), pl.ds(y, ys))
        return pltpu.make_async_remote_copy(
            src_ref=cs.at[piece], dst_ref=cr.at[piece], send_sem=c_send.at[c], recv_sem=c_recv.at[c],
            device_id=(d + 1, t), device_id_type=MESH)

    def carry_start(*which):
        @pl.when(d < n - 1)
        def _():
            for c in which:
                carry_copy(c).start()

    def carry_make(start, stop, rows):
        def plane(x, _):
            for z in range(nz):
                for r, size in rows:
                    cs[x, z, r:r + size] = fac[1, x, r:r + size, zs(z)] * adjoint(e1.at[0], coef, x, z, r, size)
            return 0

        lax.fori_loop(start, stop, plane, 0)

    def rhs_make(*which):
        @pl.when(d > 0)
        def _():
            for c in which:
                carry_copy(c).wait_recv()
            start, count = PIECES[which[0]][:2]

            def plane(x, _):
                for c in which:
                    _, _, y, ys = PIECES[c]
                    for z in range(nz):
                        here = (x + HX, z, slice(HY + y, HY + y + ys))
                        er0[here] = er0[here] + cr[x, z, y:y + ys]
                return 0

            lax.fori_loop(start, start + count, plane, 0)

    carry_make(body, rx, ((0, ry),))
    carry_start(0)
    carry_make(0, body, ((0, 8), (ry - 8, 8)))
    carry_start(1, 2)
    carry_make(0, body, ((8, ry - 16),))
    carry_start(3)
    halo_done(er0, 2, BACK)
    halo_wait(er0, 2, BACK)

    @pl.when(d < n - 1)
    def _():
        for x in range(ITERS):
            for z in range(nz):
                here = (HX + rx + x, z, slice(HY, HY + ry))
                er0[here] = er0[here] + cs[x, z]

    rhs_make(0)
    halo_start(er0, 2, AHEAD)
    rhs_make(1, 2)
    halo_start(er0, 2, ASIDE)

    def ps_late(x, _):
        for z in range(nz):
            out_ps[1, x, :, zs(z)] = wgt[1, x, :, zs(z)] * adjoint(e1.at[0], coef, x, z)
        return 0

    lax.fori_loop(0, rx, ps_late, 0)
    rhs_make(3)
    halo_wait(ec0, 1)
    halo_wait(er0, 2, AHEAD + ASIDE)
    powers(er0, ec0)
    dots(er0, ec0, 1)
    sum_start(1)
    coef0 = sum_end(1)

    def last(x, _):
        for z in range(nz):
            a = adjoint(er0, coef0, x, z)
            out_ps[0, x, :, zs(z)] = wgt[0, x, :, zs(z)] * a
            out_carry[x, :, zs(z)] = fac[0, x, :, zs(z)] * a
        return 0

    lax.fori_loop(0, rx, last, 0)
    halo_done(e1.at[0], 0)
    halo_done(e1.at[1], 3)
    halo_done(ec0, 1)
    halo_done(er0, 2, AHEAD + ASIDE)
    sum_done(0)
    sum_done(1)

    @pl.when(d < n - 1)
    def _():
        for c in range(len(PIECES)):
            carry_copy(c).wait_send()


def per_device(n, m, temp_before, temp_after, melt_phase, objective_grad, laser_path):
    steps, rx, ry, rz = temp_before.shape
    ex, ey = rx + 2 * HX, ry + 2 * HY
    nz = rz // LANES
    waves = (max(n, m) - 2).bit_length()
    f32 = jnp.float32
    vm = pl.BlockSpec(memory_space=pltpu.VMEM)
    dma = pltpu.SemaphoreType.DMA
    return pl.pallas_call(
        functools.partial(kernel, n, m),
        out_shape=(
            pltpu.VMEM((steps, rx, ry, rz), f32),
            pltpu.VMEM((rx, ry, rz), f32),
        ),
        in_specs=[pl.BlockSpec(memory_space=pl.ANY)] * 4 + [pl.BlockSpec(memory_space=pltpu.SMEM)],
        out_specs=(vm, vm),
        scratch_shapes=[
            pltpu.VMEM((2, rx, ry, rz), f32),
            pltpu.VMEM((2, rx, ry, rz), f32),
            pltpu.VMEM((2, rx, ry, rz), jnp.int32),
            pltpu.VMEM((2, ex, nz, ey, LANES), f32),
            pltpu.VMEM((ex, nz, ey, LANES), f32),
            pltpu.VMEM((ex, nz, ey, LANES), f32),
            pltpu.VMEM((ITERS - 1, ex, nz, ey, LANES), f32),
            pltpu.VMEM((2, rx, ry, rz), f32),
            pltpu.VMEM((2, rx, ry, rz), f32),
            pltpu.VMEM((rx, nz, ry, LANES), f32),
            pltpu.VMEM((rx, nz, ry, LANES), f32),
            pltpu.VMEM((2, 8, LANES), f32),
            pltpu.VMEM((2, n * m, LANES), f32),
            dma((8 + 2 * nz,)),
            dma((4, 8)), dma((4, 8)),
            dma((4,)), dma((4,)),
            dma((2,)), dma((2,)),
            pltpu.SemaphoreType.REGULAR((waves,)),
        ],
        compiler_params=pltpu.CompilerParams(
            collective_id=0, has_side_effects=True, vmem_limit_bytes=60 * 1024 * 1024
        ),
    )(temp_before, temp_after, melt_phase, objective_grad, laser_path)


def solution(mesh):
    spec = P(None, "scan", "track", None)
    return jax.shard_map(
        functools.partial(per_device, mesh.shape["scan"], mesh.shape["track"]),
        mesh=mesh,
        in_specs=(spec, spec, spec, spec, P()),
        out_specs=(spec, P("scan", "track", None)),
        check_vma=False,
    )
```

```python
import functools

import jax
import jax.numpy as jnp
from jax import lax
from jax.experimental import pallas as pl
from jax.experimental.pallas import tpu as pltpu
from jax.sharding import PartitionSpec as P

ITERS = 4
CAPS = (0.6, 2.0, 0.9)
ABSORBS = (0.35, 0.5, 0.65)
spot_radius = 3.0
decay_depth = 4.0
spot_peak = 4.0

SHIFT = 7.25
SCALE = 3.0

HX = 4
HY = 8

DIRS = tuple((dx, dy) for dx in (-1, 0, 1) for dy in (-1, 0, 1) if (dx, dy) != (0, 0))
BACK = ((-1, 0),)
AHEAD = ((1, -1), (1, 0), (1, 1))
ASIDE = ((0, -1), (0, 1))
PAIRS = tuple((i, j) for i in range(ITERS) for j in range(i, ITERS)) + ((ITERS - 1, ITERS),)
MESH = pl.DeviceIdType.MESH
LANES = 128
TRIPS = 2
DOT_TRIPS = 4
WRITES = 4


def lookup(melt, values):
    return jnp.where(
        melt == 0,
        jnp.float32(values[0]),
        jnp.where(melt == 1, jnp.float32(values[1]), jnp.float32(values[2])),
    )


def solve_small(g):
    def gram(i, j):
        return g[(min(i, j), max(i, j))]

    n = ITERS
    h = {}
    for i in range(n):
        for j in range(i, n):
            value = SCALE * gram(i + 1, j) + SHIFT * gram(i, j)
            if i > 0:
                value = value + SCALE * gram(i - 1, j)
            h[(i, j)] = value
    low, inv, y = {}, {}, {}
    for j in range(n):
        d = h[(j, j)]
        for k in range(j):
            d = d - low[(j, k)] * low[(j, k)] * inv[("d", k)]
        good = d > 1e-7 * h[(j, j)]
        inv[("d", j)] = jnp.where(good, d, 0.0)
        inv[j] = jnp.where(good, 1.0 / jnp.where(good, d, 1.0), 0.0)
        for i in range(j + 1, n):
            t = h[(j, i)]
            for k in range(j):
                t = t - low[(i, k)] * low[(j, k)] * inv[("d", k)]
            low[(i, j)] = t * inv[j]
    for i in range(n):
        t = gram(0, i)
        for k in range(i):
            t = t - low[(i, k)] * y[k]
        y[i] = t
    a = [None] * n
    for i in reversed(range(n)):
        t = y[i] * inv[i]
        for k in range(i + 1, n):
            t = t - low[(k, i)] * a[k]
        a[i] = t
    return a


def kernel(n, m, tb_in, ta_in, melt_in, grad_in, path, ps_late, er0, v, fac, wgt, weights_out,
           tb, ta, melt, e1, ec0, cs, cr, part, red,
           load_sem, h_send, h_recv, c_send, c_recv, r_send, r_recv, known):
    rx, ry, rz = tb.shape[1:]
    ex, ey = rx + 2 * HX, ry + 2 * HY
    nz = rz // LANES
    d = lax.axis_index("scan")
    t = lax.axis_index("track")

    def exists(dx, dy):
        ok = None
        if dx < 0:
            ok = d > 0
        if dx > 0:
            ok = d < n - 1
        if dy != 0:
            oky = (t > 0) if dy < 0 else (t < m - 1)
            ok = oky if ok is None else jnp.logical_and(ok, oky)
        return ok

    def at_distance(r):
        for dx, dy in DIRS:
            ok = None
            if dx != 0:
                ok = (d >= r) if dx < 0 else (d < n - r)
            if dy != 0:
                oky = (t >= r) if dy < 0 else (t < m - r)
                ok = oky if ok is None else jnp.logical_and(ok, oky)
            if (dx == 0 or r < n) and (dy == 0 or r < m):
                yield ok, (d + dx * r, t + dy * r)

    def greet(sem, r):
        for ok, device in at_distance(r):
            @pl.when(ok)
            def _(device=device):
                pl.semaphore_signal(sem, inc=1, device_id=device, device_id_type=MESH)

    def greeted(sem, r):
        count = jnp.int32(0)
        for ok, _ in at_distance(r):
            count = count + ok.astype(jnp.int32)
        pl.semaphore_wait(sem, count)

    barrier = pltpu.get_barrier_semaphore()
    greet(barrier, 1)

    def zero_halo(ref):
        @pl.when(d == 0)
        def _():
            ref[0:HX] = jnp.zeros((HX, nz, ey, LANES), jnp.float32)

        @pl.when(d == n - 1)
        def _():
            ref[ex - HX:ex] = jnp.zeros((HX, nz, ey, LANES), jnp.float32)

        @pl.when(t == 0)
        def _():
            ref[:, :, 0:HY] = jnp.zeros((ex, nz, HY, LANES), jnp.float32)

        @pl.when(t == m - 1)
        def _():
            ref[:, :, ey - HY:ey] = jnp.zeros((ex, nz, HY, LANES), jnp.float32)

    def zs(z):
        return slice(z * LANES, (z + 1) * LANES)

    loads = []
    for q, (s, kind) in enumerate([(1, 2), (1, 0), (1, 1), (1, 3), (0, 0), (0, 1), (0, 2), (0, 3)]):
        if kind == 2:
            where = e1.at[0] if s == 1 else er0
            parts = [
                pltpu.make_async_copy(
                    grad_in.at[s, :, :, pl.ds(z * LANES, LANES)],
                    where.at[pl.ds(HX, rx), z, pl.ds(HY, ry)],
                    load_sem.at[8 + s * nz + z],
                )
                for z in range(nz)
            ]
        else:
            src, dst = ((tb_in, tb), (melt_in, melt), None, (ta_in, ta))[kind]
            parts = [pltpu.make_async_copy(src.at[s], dst.at[s], load_sem.at[q])]
        loads.append(parts)

    def loaded(*which):
        for q in which:
            for c in loads[q]:
                c.wait()

    for parts in loads:
        for c in parts:
            c.start()
    zero_halo(e1.at[0])
    zero_halo(er0)

    def terms(s, x):
        base = lookup(melt[s, x], CAPS)
        h = jnp.tanh(tb[s, x])
        return base * (1.0 + 0.5 * h), base, h

    def diagonals(s, cap_ref):
        def body(x, _):
            cap, _, _ = terms(s, x)
            cap = (cap + (6.0 - SHIFT)) * (1.0 / SCALE)
            for z in range(nz):
                cap_ref[x + HX, z, HY:HY + ry] = cap[:, zs(z)]
            return 0

        lax.fori_loop(0, rx, body, 0)

    def factors(s):
        def body(x, _):
            cap, base, h = terms(s, x)
            slope = base * 0.5 * (1.0 - h * h)
            fac[s, x] = cap - slope * (ta[s, x] - tb[s, x])
            return 0

        lax.fori_loop(0, rx, body, 0)

    waves = known.shape[0]

    def spread(step):
        if 0 < step <= waves:
            greeted(known.at[step - 1], 2 ** (step - 1))
        if step < waves:
            greet(known.at[step], 2 ** step)
        return step + 1

    loaded(0)
    greeted(barrier, 1)

    def span(delta, low, count, width):
        if delta == 0:
            return low, low, count
        if delta > 0:
            return low + count - width, low - width, width
        return low, low + count, width

    def halo_copy(ref, which, q):
        dx, dy = DIRS[q]
        wide = ITERS if which in (0, 2) else ITERS - 1
        if dx != 0 and dy != 0:
            wx = wy = wide - 2 if dx > 0 and dy > 0 else wide - 1
        else:
            wx = wide - 1 if dx > 0 else wide
            wy = wide - 1 if dy > 0 else wide
        x_src, x_dst, x_size = span(dx, HX, rx, wx)
        y_src, y_dst, y_size = span(dy, HY, ry, wy)
        if which == 2 and dx == 0:
            x_size = rx + ITERS - 1
        return pltpu.make_async_remote_copy(
            src_ref=ref.at[pl.ds(x_src, x_size), slice(None), pl.ds(y_src, y_size)],
            dst_ref=ref.at[pl.ds(x_dst, x_size), slice(None), pl.ds(y_dst, y_size)],
            send_sem=h_send.at[which, q],
            recv_sem=h_recv.at[which, q],
            device_id=(d + dx, t + dy),
            device_id_type=MESH,
        )

    def halo_start(ref, which, wanted=DIRS):
        for q, (dx, dy) in enumerate(DIRS):
            if (dx, dy) in wanted:
                @pl.when(exists(dx, dy))
                def _(q=q):
                    halo_copy(ref, which, q).start()

    def halo_wait(ref, which, wanted=DIRS):
        for q, (dx, dy) in enumerate(DIRS):
            if (dx, dy) in wanted:
                @pl.when(exists(-dx, -dy))
                def _(q=q):
                    halo_copy(ref, which, q).wait_recv()

    def halo_done(ref, which, wanted=DIRS):
        for q, (dx, dy) in enumerate(DIRS):
            if (dx, dy) in wanted:
                @pl.when(exists(dx, dy))
                def _(q=q):
                    halo_copy(ref, which, q).wait_send()

    lane8 = lax.broadcasted_iota(jnp.int32, (8, LANES), 1)
    first, final = lane8 == 0, lane8 == LANES - 1

    def powers(v0, cap_ref):
        at = [v0] + [v.at[k] for k in range(ITERS - 1)]
        for k in range(ITERS - 1):
            tiles = range(HY - 4, HY + ry + 4, 8)
            start, count = HX - ITERS + 2 + k, rx + 2 * (ITERS - 2 - k) + 1
            trips = 3 if count % 3 == 0 else TRIPS
            if count % trips:
                start, count = start - 1, count + 1
            planes = count // trips

            def trip(p, _, k=k, tiles=tiles, planes=planes, start=start):
                x = start + planes * p
                for r in tiles:
                    c = [[at[k][x + q, z, r:r + 8] for z in range(nz)] for q in range(-1, planes + 1)]
                    for q in range(planes):
                        mid = c[q + 1]
                        up = [pltpu.roll(w, 1, 1) for w in mid]
                        down = [pltpu.roll(w, LANES - 1, 1) for w in mid]
                        for z in range(nz):
                            above = jnp.where(first, up[z - 1] if z > 0 else 0.0, up[z])
                            below = jnp.where(final, down[z + 1] if z < nz - 1 else 0.0, down[z])
                            beside = (c[q][z] + c[q + 2][z]) + (above + below)
                            beside = beside + (at[k][x + q, z, r - 1:r + 7] + at[k][x + q, z, r + 1:r + 9])
                            new = cap_ref[x + q, z, r:r + 8] * mid[z] - beside * (1.0 / SCALE)
                            if k > 0:
                                new = new - at[k - 1][x + q, z, r:r + 8]
                            at[k + 1][x + q, z, r:r + 8] = new
                return 0

            lax.fori_loop(0, trips, trip, 0)
            zero_halo(at[k + 1])

    def dots(v0, cap_ref, slot):
        at = [v0] + [v.at[k] for k in range(ITERS - 1)]
        group = max(1, rx // DOT_TRIPS)

        def body(p, acc):
            acc = list(acc)
            for g in range(group):
                x = HX + p * group + g
                for r in range(HY, HY + ry, 8):
                    tips = [at[-1][x, z, r:r + 8] for z in range(nz)]
                    for z in range(nz):
                        vals = [ref[x, z, r:r + 8] for ref in at[:-1]] + [tips[z]]
                        over = tips[z + 1] if z < nz - 1 else 0.0
                        below = pltpu.roll(jnp.where(first, over, tips[z]), LANES - 1, 1)
                        after = at[-1][x + 1, z, r:r + 8] + at[-1][x, z, r + 1:r + 9] + below
                        vals.append(cap_ref[x, z, r:r + 8] * tips[z] - after * (2.0 / SCALE))
                        for q, (i, j) in enumerate(PAIRS):
                            acc[q] = acc[q] + vals[i] * vals[j]
            return tuple(acc)

        acc = lax.fori_loop(0, rx // group, body, tuple(jnp.zeros((8, LANES), jnp.float32) for _ in PAIRS))
        lane = lax.broadcasted_iota(jnp.int32, (1, LANES), 1)
        row = jnp.zeros((1, LANES), jnp.float32)
        for q, a in enumerate(acc):
            s = jnp.sum(jnp.sum(a, axis=0, keepdims=True), axis=1, keepdims=True)
            row = jnp.where(lane == q, s, row)
        part[slot, 0:1] = row

    me = d * m + t
    others = n * m - 1

    def sum_copy(slot, device):
        return pltpu.make_async_remote_copy(
            src_ref=part.at[slot, pl.ds(0, 1)],
            dst_ref=red.at[slot, pl.ds(me, 1)],
            send_sem=r_send.at[slot],
            recv_sem=r_recv.at[slot],
            device_id=device,
            device_id_type=MESH,
        )

    def sum_start(slot):
        for j in range(m):
            row = jnp.where(2 * t < m, m - 1 - j, j)
            for k in range(n):
                column = lax.rem(d + (n // 2 + k) % n, n)
                if (n // 2 + k) % n == 0:
                    @pl.when(row != t)
                    def _(row=row):
                        sum_copy(slot, (d, row)).start()
                else:
                    sum_copy(slot, (column, row)).start()
        red[slot, pl.ds(me, 1)] = part[slot, 0:1]

    def all_others(ref, sem):
        view = ref.at[pl.ds(0, others)]
        pltpu.make_async_copy(view, view, sem).wait()

    def sum_end(slot):
        all_others(red.at[slot], r_recv.at[slot])
        total = jnp.sum(red[slot], axis=0, keepdims=True)
        lane = lax.broadcasted_iota(jnp.int32, (1, LANES), 1)
        g = {}
        for q, pair in enumerate(PAIRS):
            g[pair] = jnp.sum(jnp.where(lane == q, total, 0.0), axis=1, keepdims=True)
        g[PAIRS[-1]] = g[PAIRS[-1]] - g[(ITERS - 2, ITERS - 1)]
        return solve_small(g)

    def sum_done(slot):
        all_others(red.at[slot], r_send.at[slot])

    def adjoint(v0, coef, x, z, r=0, size=None):
        rows = slice(HY + r, HY + r + (size or ry))
        out = coef[0] * v0[x + HX, z, rows]
        for k in range(1, ITERS):
            out = out + coef[k] * v[k - 1, x + HX, z, rows]
        return out

    def weights(s):
        width = m * ry
        yy = (t * ry + lax.broadcasted_iota(jnp.int32, (ry, 128), 0)).astype(jnp.float32)
        xx = (d * rx + lax.broadcasted_iota(jnp.int32, (ry, 128), 1)).astype(jnp.float32)
        two = 2.0 * spot_radius * spot_radius
        surface = jnp.zeros((ry, 128), jnp.float32)
        for k in range(path.shape[1]):
            cell = path[s, k]
            dx = xx - lax.div(cell, jnp.int32(width)).astype(jnp.float32)
            dy = yy - lax.rem(cell, jnp.int32(width)).astype(jnp.float32)
            surface = surface + jnp.exp(-dx * dx / two) * jnp.exp(-dy * dy / two)
        zz = lax.broadcasted_iota(jnp.int32, (1, rz), 1).astype(jnp.float32)
        fall = spot_peak * jnp.exp(-zz / decay_depth)
        lane = lax.broadcasted_iota(jnp.int32, (ry, 128), 1)

        def body(x, _):
            column = jnp.sum(jnp.where(lane == x, surface, 0.0), axis=1, keepdims=True)
            wgt[s, x] = lookup(melt[s, x], ABSORBS) * (1.0 + column * fall)
            return 0

        lax.fori_loop(0, rx, body, 0)

    halo_start(e1.at[0], 0)
    step = spread(0)
    loaded(1, 2)
    diagonals(1, e1.at[1])
    halo_start(e1.at[1], 3)
    step = spread(step)
    loaded(4, 5)
    diagonals(0, ec0)
    halo_start(ec0, 1)
    step = spread(step)
    loaded(3)
    factors(1)
    loaded(7)
    factors(0)
    while step < waves:
        step = spread(step)
    spread(step)
    halo_wait(e1.at[0], 0)
    halo_wait(e1.at[1], 3)
    powers(e1.at[0], e1.at[1])
    dots(e1.at[0], e1.at[1], 0)
    sum_start(0)
    loaded(6)
    halo_start(er0, 2, BACK)
    weights(1)
    weights(0)
    coef = sum_end(0)

    tail = ITERS - 1
    body = rx - tail
    PIECES = ((body, tail, 0, ry), (0, body, 0, ITERS), (0, body, ry - tail, tail), (0, body, ITERS, ry - tail - ITERS))

    def carry_copy(c):
        x, xs, y, ys = PIECES[c]
        piece = (pl.ds(x, xs), slice(None), pl.ds(y, ys))
        return pltpu.make_async_remote_copy(
            src_ref=cs.at[piece], dst_ref=cr.at[piece], send_sem=c_send.at[c], recv_sem=c_recv.at[c],
            device_id=(d + 1, t), device_id_type=MESH)

    def carry_start(*which):
        @pl.when(d < n - 1)
        def _():
            for c in which:
                carry_copy(c).start()

    def carry_make(start, stop, rows):
        def plane(x, _):
            for z in range(nz):
                for r, size in rows:
                    cs[x, z, r:r + size] = fac[1, x, r:r + size, zs(z)] * adjoint(e1.at[0], coef, x, z, r, size)
            return 0

        lax.fori_loop(start, stop, plane, 0)

    def rhs_make(*which):
        @pl.when(d > 0)
        def _():
            for c in which:
                carry_copy(c).wait_recv()
            start, count = PIECES[which[0]][:2]

            def plane(x, _):
                for c in which:
                    _, _, y, ys = PIECES[c]
                    for z in range(nz):
                        here = (x + HX, z, slice(HY + y, HY + y + ys))
                        er0[here] = er0[here] + cr[x, z, y:y + ys]
                return 0

            lax.fori_loop(start, start + count, plane, 0)

    carry_make(body, rx, ((0, ry),))
    carry_start(0)
    carry_make(0, body, ((0, 8), (ry - 8, 8)))
    carry_start(1, 2)
    carry_make(0, body, ((8, ry - 16),))
    carry_start(3)
    halo_done(er0, 2, BACK)
    halo_wait(er0, 2, BACK)

    @pl.when(d < n - 1)
    def _():
        for x in range(ITERS):
            for z in range(nz):
                here = (HX + rx + x, z, slice(HY, HY + ry))
                er0[here] = er0[here] + cs[x, z]

    rhs_make(0)
    halo_start(er0, 2, AHEAD)
    rhs_make(1, 2)
    halo_start(er0, 2, ASIDE)

    def late(x, _):
        for z in range(nz):
            ps_late[x, :, zs(z)] = wgt[1, x, :, zs(z)] * adjoint(e1.at[0], coef, x, z)
        return 0

    lax.fori_loop(0, rx, late, 0)
    rhs_make(3)
    halo_wait(ec0, 1)
    halo_wait(er0, 2, AHEAD + ASIDE)
    powers(er0, ec0)
    dots(er0, ec0, 1)
    sum_start(1)
    halo_done(e1.at[0], 0)
    halo_done(e1.at[1], 3)
    halo_done(ec0, 1)
    halo_done(er0, 2, AHEAD + ASIDE)
    sum_done(0)

    @pl.when(d < n - 1)
    def _():
        for c in range(len(PIECES)):
            carry_copy(c).wait_send()

    coef0 = sum_end(1)
    for k in range(ITERS):
        weights_out[k] = jnp.broadcast_to(coef0[k], (8, LANES))
    sum_done(1)


def finish(ps_late, e, v, fac, wgt, coef, out_ps, out_carry, ps, carry, sems):
    rx, ry, rz = ps.shape
    nz = rz // LANES
    late = pltpu.make_async_copy(ps_late, out_ps.at[1], sems.at[0])
    late.start()
    part = max(1, rx // WRITES)
    c = [coef[k] for k in range(ITERS)]
    copies = [late]
    for q, low in enumerate(range(0, rx, part)):
        size = min(part, rx - low)

        def plane(x, _):
            for z in range(nz):
                lanes = slice(z * LANES, (z + 1) * LANES)
                for r in range(0, ry, 8):
                    rows = slice(HY + r, HY + r + 8)
                    a = c[0] * e[x + HX, z, rows]
                    for k in range(1, ITERS):
                        a = a + c[k] * v[k - 1, x + HX, z, rows]
                    ps[x, r:r + 8, lanes] = wgt[0, x, r:r + 8, lanes] * a
                    carry[x, r:r + 8, lanes] = fac[0, x, r:r + 8, lanes] * a
            return 0

        lax.fori_loop(low, low + size, plane, 0)
        piece = pl.ds(low, size)
        copies.append(pltpu.make_async_copy(ps.at[piece], out_ps.at[0, piece], sems.at[1 + 2 * q]))
        copies.append(pltpu.make_async_copy(carry.at[piece], out_carry.at[piece], sems.at[2 + 2 * q]))
        copies[-2].start()
        copies[-1].start()
    for copy in copies:
        copy.wait()


def per_device(n, m, temp_before, temp_after, melt_phase, objective_grad, laser_path):
    steps, rx, ry, rz = temp_before.shape
    ex, ey = rx + 2 * HX, ry + 2 * HY
    nz = rz // LANES
    waves = (max(n, m) - 2).bit_length()
    f32 = jnp.float32
    vm = pl.BlockSpec(memory_space=pltpu.VMEM)
    dma = pltpu.SemaphoreType.DMA
    results = pl.pallas_call(
        functools.partial(kernel, n, m),
        out_shape=tuple(
            pltpu.VMEM(shape, f32)
            for shape in (
                (rx, ry, rz),
                (ex, nz, ey, LANES),
                (ITERS - 1, ex, nz, ey, LANES),
                (steps, rx, ry, rz),
                (steps, rx, ry, rz),
                (ITERS, 8, LANES),
            )
        ),
        in_specs=[pl.BlockSpec(memory_space=pl.ANY)] * 4 + [pl.BlockSpec(memory_space=pltpu.SMEM)],
        out_specs=(vm,) * 6,
        scratch_shapes=[
            pltpu.VMEM((2, rx, ry, rz), f32),
            pltpu.VMEM((2, rx, ry, rz), f32),
            pltpu.VMEM((2, rx, ry, rz), jnp.int32),
            pltpu.VMEM((2, ex, nz, ey, LANES), f32),
            pltpu.VMEM((ex, nz, ey, LANES), f32),
            pltpu.VMEM((rx, nz, ry, LANES), f32),
            pltpu.VMEM((rx, nz, ry, LANES), f32),
            pltpu.VMEM((2, 8, LANES), f32),
            pltpu.VMEM((2, n * m, LANES), f32),
            dma((8 + 2 * nz,)),
            dma((4, 8)), dma((4, 8)),
            dma((4,)), dma((4,)),
            dma((2,)), dma((2,)),
            pltpu.SemaphoreType.REGULAR((waves,)),
        ],
        compiler_params=pltpu.CompilerParams(
            collective_id=0, has_side_effects=True, vmem_limit_bytes=56 * 1024 * 1024
        ),
    )(temp_before, temp_after, melt_phase, objective_grad, laser_path)
    hbm = pl.BlockSpec(memory_space=pl.ANY)
    parts = -(-rx // max(1, rx // WRITES))
    return pl.pallas_call(
        finish,
        out_shape=(
            jax.ShapeDtypeStruct((steps, rx, ry, rz), f32),
            jax.ShapeDtypeStruct((rx, ry, rz), f32),
        ),
        in_specs=[vm] * 6,
        out_specs=(hbm, hbm),
        scratch_shapes=[pltpu.VMEM((rx, ry, rz), f32), pltpu.VMEM((rx, ry, rz), f32), dma((1 + 2 * parts,))],
        compiler_params=pltpu.CompilerParams(vmem_limit_bytes=4 * 1024 * 1024),
    )(*results)


def solution(mesh):
    spec = P(None, "scan", "track", None)
    return jax.shard_map(
        functools.partial(per_device, mesh.shape["scan"], mesh.shape["track"]),
        mesh=mesh,
        in_specs=(spec, spec, spec, spec, P()),
        out_specs=(spec, P("scan", "track", None)),
        check_vma=False,
    )
```

```python
import functools

import jax
import jax.numpy as jnp
from jax import lax
from jax.experimental import pallas as pl
from jax.experimental.pallas import tpu as pltpu
from jax.sharding import PartitionSpec as P

ITERS = 4
CAPS = (0.6, 2.0, 0.9)
ABSORBS = (0.35, 0.5, 0.65)
spot_radius = 3.0
decay_depth = 4.0
spot_peak = 4.0

SHIFT = 7.25
SCALE = 3.0

HX = 4
HY = 8

DIRS = ((-1, 0), (1, 0), (-1, -1), (-1, 1), (1, -1), (1, 1), (0, -1), (0, 1))
BACK = ((-1, 0),)
AHEAD = ((1, -1), (1, 0), (1, 1))
ASIDE = ((0, -1), (0, 1))
PAIRS = tuple((i, j) for i in range(ITERS) for j in range(i, ITERS)) + ((ITERS - 1, ITERS),)
MESH = pl.DeviceIdType.MESH
LANES = 128
TRIPS = 2
DOT_TRIPS = 4
WRITES = 4


def lookup(melt, values):
    return jnp.where(
        melt == 0,
        jnp.float32(values[0]),
        jnp.where(melt == 1, jnp.float32(values[1]), jnp.float32(values[2])),
    )


def solve_small(g):
    def gram(i, j):
        return g[(min(i, j), max(i, j))]

    n = ITERS
    h = {}
    for i in range(n):
        for j in range(i, n):
            value = SCALE * gram(i + 1, j) + SHIFT * gram(i, j)
            if i > 0:
                value = value + SCALE * gram(i - 1, j)
            h[(i, j)] = value
    low, inv, y = {}, {}, {}
    for j in range(n):
        d = h[(j, j)]
        for k in range(j):
            d = d - low[(j, k)] * low[(j, k)] * inv[("d", k)]
        good = d > 1e-7 * h[(j, j)]
        inv[("d", j)] = jnp.where(good, d, 0.0)
        inv[j] = jnp.where(good, 1.0 / jnp.where(good, d, 1.0), 0.0)
        for i in range(j + 1, n):
            t = h[(j, i)]
            for k in range(j):
                t = t - low[(i, k)] * low[(j, k)] * inv[("d", k)]
            low[(i, j)] = t * inv[j]
    for i in range(n):
        t = gram(0, i)
        for k in range(i):
            t = t - low[(i, k)] * y[k]
        y[i] = t
    a = [None] * n
    for i in reversed(range(n)):
        t = y[i] * inv[i]
        for k in range(i + 1, n):
            t = t - low[(k, i)] * a[k]
        a[i] = t
    return a


def kernel(n, m, tb_in, ta_in, melt_in, grad_in, path, ps_late, er0, v, fac, wgt, weights_out,
           tb, ta, melt, e1, ec0, cs, cr, part, red,
           load_sem, h_send, h_recv, c_send, c_recv, r_send, r_recv, known):
    rx, ry, rz = tb.shape[1:]
    ex, ey = rx + 2 * HX, ry + 2 * HY
    nz = rz // LANES
    d = lax.axis_index("scan")
    t = lax.axis_index("track")

    def exists(dx, dy):
        ok = None
        if dx < 0:
            ok = d > 0
        if dx > 0:
            ok = d < n - 1
        if dy != 0:
            oky = (t > 0) if dy < 0 else (t < m - 1)
            ok = oky if ok is None else jnp.logical_and(ok, oky)
        return ok

    def at_distance(r):
        for dx, dy in DIRS:
            ok = None
            if dx != 0:
                ok = (d >= r) if dx < 0 else (d < n - r)
            if dy != 0:
                oky = (t >= r) if dy < 0 else (t < m - r)
                ok = oky if ok is None else jnp.logical_and(ok, oky)
            if (dx == 0 or r < n) and (dy == 0 or r < m):
                yield ok, (d + dx * r, t + dy * r)

    def greet(sem, r):
        for ok, device in at_distance(r):
            @pl.when(ok)
            def _(device=device):
                pl.semaphore_signal(sem, inc=1, device_id=device, device_id_type=MESH)

    def greeted(sem, r):
        count = jnp.int32(0)
        for ok, _ in at_distance(r):
            count = count + ok.astype(jnp.int32)
        pl.semaphore_wait(sem, count)

    barrier = pltpu.get_barrier_semaphore()
    greet(barrier, 1)

    def zero_halo(ref):
        @pl.when(d == 0)
        def _():
            ref[0:HX] = jnp.zeros((HX, nz, ey, LANES), jnp.float32)

        @pl.when(d == n - 1)
        def _():
            ref[ex - HX:ex] = jnp.zeros((HX, nz, ey, LANES), jnp.float32)

        @pl.when(t == 0)
        def _():
            ref[:, :, 0:HY] = jnp.zeros((ex, nz, HY, LANES), jnp.float32)

        @pl.when(t == m - 1)
        def _():
            ref[:, :, ey - HY:ey] = jnp.zeros((ex, nz, HY, LANES), jnp.float32)

    def zs(z):
        return slice(z * LANES, (z + 1) * LANES)

    loads = []
    for q, (s, kind) in enumerate([(1, 2), (1, 0), (1, 1), (1, 3), (0, 0), (0, 1), (0, 2), (0, 3)]):
        if kind == 2:
            where = e1.at[0] if s == 1 else er0
            parts = [
                pltpu.make_async_copy(
                    grad_in.at[s, :, :, pl.ds(z * LANES, LANES)],
                    where.at[pl.ds(HX, rx), z, pl.ds(HY, ry)],
                    load_sem.at[8 + s * nz + z],
                )
                for z in range(nz)
            ]
        else:
            src, dst = ((tb_in, tb), (melt_in, melt), None, (ta_in, ta))[kind]
            parts = [pltpu.make_async_copy(src.at[s], dst.at[s], load_sem.at[q])]
        loads.append(parts)

    def loaded(*which):
        for q in which:
            for c in loads[q]:
                c.wait()

    for c in loads[0]:
        c.start()
    zero_halo(e1.at[0])
    zero_halo(er0)

    def terms(s, x):
        base = lookup(melt[s, x], CAPS)
        h = jnp.tanh(tb[s, x])
        return base * (1.0 + 0.5 * h), base, h

    def diagonals(s, cap_ref):
        def body(x, _):
            cap, _, _ = terms(s, x)
            cap = (cap + (6.0 - SHIFT)) * (1.0 / SCALE)
            for z in range(nz):
                cap_ref[x + HX, z, HY:HY + ry] = cap[:, zs(z)]
            return 0

        lax.fori_loop(0, rx, body, 0)

    def factors(s):
        def body(x, _):
            cap, base, h = terms(s, x)
            slope = base * 0.5 * (1.0 - h * h)
            fac[s, x] = cap - slope * (ta[s, x] - tb[s, x])
            return 0

        lax.fori_loop(0, rx, body, 0)

    waves = known.shape[0]

    def spread(step):
        if 0 < step <= waves:
            greeted(known.at[step - 1], 2 ** (step - 1))
        if step < waves:
            greet(known.at[step], 2 ** step)
        return step + 1

    loaded(0)
    for parts in loads[1:]:
        for c in parts:
            c.start()
    greeted(barrier, 1)

    def span(delta, low, count, width):
        if delta == 0:
            return low, low, count
        if delta > 0:
            return low + count - width, low - width, width
        return low, low + count, width

    def halo_copy(ref, which, q):
        dx, dy = DIRS[q]
        wide = ITERS if which in (0, 2) else ITERS - 1
        if dx != 0 and dy != 0:
            wx = wy = wide - 2 if dx > 0 and dy > 0 else wide - 1
        else:
            wx = wide - 1 if dx > 0 else wide
            wy = wide - 1 if dy > 0 else wide
        x_src, x_dst, x_size = span(dx, HX, rx, wx)
        y_src, y_dst, y_size = span(dy, HY, ry, wy)
        if which == 2 and dx == 0:
            x_size = rx + ITERS - 1
        return pltpu.make_async_remote_copy(
            src_ref=ref.at[pl.ds(x_src, x_size), slice(None), pl.ds(y_src, y_size)],
            dst_ref=ref.at[pl.ds(x_dst, x_size), slice(None), pl.ds(y_dst, y_size)],
            send_sem=h_send.at[which, q],
            recv_sem=h_recv.at[which, q],
            device_id=(d + dx, t + dy),
            device_id_type=MESH,
        )

    def halo_start(ref, which, wanted=DIRS):
        for q, (dx, dy) in enumerate(DIRS):
            if (dx, dy) in wanted:
                @pl.when(exists(dx, dy))
                def _(q=q):
                    halo_copy(ref, which, q).start()

    def halo_wait(ref, which, wanted=DIRS):
        for q, (dx, dy) in enumerate(DIRS):
            if (dx, dy) in wanted:
                @pl.when(exists(-dx, -dy))
                def _(q=q):
                    halo_copy(ref, which, q).wait_recv()

    def halo_done(ref, which, wanted=DIRS):
        for q, (dx, dy) in enumerate(DIRS):
            if (dx, dy) in wanted:
                @pl.when(exists(dx, dy))
                def _(q=q):
                    halo_copy(ref, which, q).wait_send()

    lane8 = lax.broadcasted_iota(jnp.int32, (8, LANES), 1)
    first, final = lane8 == 0, lane8 == LANES - 1

    def advance(v0, cap_ref, k, start, count, tiles):
        at = [v0] + [v.at[q] for q in range(ITERS - 1)]
        trips = TRIPS if count % TRIPS == 0 and count > 4 else 1
        planes = count // trips

        def trip(p, _):
            x = start + planes * p
            for r in tiles:
                c = [[at[k][x + q, z, r:r + 8] for z in range(nz)] for q in range(-1, planes + 1)]
                for q in range(planes):
                    mid = c[q + 1]
                    up = [pltpu.roll(w, 1, 1) for w in mid]
                    down = [pltpu.roll(w, LANES - 1, 1) for w in mid]
                    for z in range(nz):
                        above = jnp.where(first, up[z - 1] if z > 0 else 0.0, up[z])
                        below = jnp.where(final, down[z + 1] if z < nz - 1 else 0.0, down[z])
                        beside = (c[q][z] + c[q + 2][z]) + (above + below)
                        beside = beside + (at[k][x + q, z, r - 1:r + 7] + at[k][x + q, z, r + 1:r + 9])
                        new = cap_ref[x + q, z, r:r + 8] * mid[z] - beside * (1.0 / SCALE)
                        if k > 0:
                            new = new - at[k - 1][x + q, z, r:r + 8]
                        at[k + 1][x + q, z, r:r + 8] = new
            return 0

        if trips == 1:
            trip(0, 0)
        else:
            lax.fori_loop(0, trips, trip, 0)

    def inner_part(k):
        low, high = HY + 4 + k, HY + ry - 4 - k
        return low, high, [min(r, high - 8) for r in range(low, high, 8)]

    def powers_inside(v0, cap_ref):
        for k in range(ITERS - 1):
            advance(v0, cap_ref, k, HX + 1 + k, rx - 2 - 2 * k, inner_part(k)[2])

    def powers_around(v0, cap_ref):
        for k in range(ITERS - 1):
            low, high, tiles = inner_part(k)
            edge = [low - 8, high]
            first_plane = HX - (ITERS - 2) + k
            advance(v0, cap_ref, k, first_plane, HX + 1 + k - first_plane, edge[:1] + tiles + edge[1:])
            advance(v0, cap_ref, k, HX + rx - 1 - k, ITERS, edge[:1] + tiles + edge[1:])
            advance(v0, cap_ref, k, HX + 1 + k, rx - 2 - 2 * k, edge)
            zero_halo(v.at[k])

    def dots(v0, cap_ref, slot):
        at = [v0] + [v.at[k] for k in range(ITERS - 1)]
        group = max(1, rx // DOT_TRIPS)

        def body(p, acc):
            acc = list(acc)
            for g in range(group):
                x = HX + p * group + g
                for r in range(HY, HY + ry, 8):
                    tips = [at[-1][x, z, r:r + 8] for z in range(nz)]
                    for z in range(nz):
                        vals = [ref[x, z, r:r + 8] for ref in at[:-1]] + [tips[z]]
                        over = tips[z + 1] if z < nz - 1 else 0.0
                        below = pltpu.roll(jnp.where(first, over, tips[z]), LANES - 1, 1)
                        after = at[-1][x + 1, z, r:r + 8] + at[-1][x, z, r + 1:r + 9] + below
                        vals.append(cap_ref[x, z, r:r + 8] * tips[z] - after * (2.0 / SCALE))
                        for q, (i, j) in enumerate(PAIRS):
                            acc[q] = acc[q] + vals[i] * vals[j]
            return tuple(acc)

        acc = lax.fori_loop(0, rx // group, body, tuple(jnp.zeros((8, LANES), jnp.float32) for _ in PAIRS))
        lane = lax.broadcasted_iota(jnp.int32, (1, LANES), 1)
        row = jnp.zeros((1, LANES), jnp.float32)
        for q, a in enumerate(acc):
            s = jnp.sum(jnp.sum(a, axis=0, keepdims=True), axis=1, keepdims=True)
            row = jnp.where(lane == q, s, row)
        part[slot, 0:1] = row

    me = d * m + t
    others = n * m - 1

    def sum_copy(slot, device):
        return pltpu.make_async_remote_copy(
            src_ref=part.at[slot, pl.ds(0, 1)],
            dst_ref=red.at[slot, pl.ds(me, 1)],
            send_sem=r_send.at[slot],
            recv_sem=r_recv.at[slot],
            device_id=device,
            device_id_type=MESH,
        )

    def sum_start(slot):
        for j in range(m):
            row = jnp.where(2 * t < m, m - 1 - j, j)
            for k in range(n):
                column = lax.rem(d + (n // 2 + k) % n, n)
                if (n // 2 + k) % n == 0:
                    @pl.when(row != t)
                    def _(row=row):
                        sum_copy(slot, (d, row)).start()
                else:
                    sum_copy(slot, (column, row)).start()
        red[slot, pl.ds(me, 1)] = part[slot, 0:1]

    def all_others(ref, sem):
        view = ref.at[pl.ds(0, others)]
        pltpu.make_async_copy(view, view, sem).wait()

    def sum_end(slot):
        all_others(red.at[slot], r_recv.at[slot])
        total = jnp.sum(red[slot], axis=0, keepdims=True)
        lane = lax.broadcasted_iota(jnp.int32, (1, LANES), 1)
        g = {}
        for q, pair in enumerate(PAIRS):
            g[pair] = jnp.sum(jnp.where(lane == q, total, 0.0), axis=1, keepdims=True)
        g[PAIRS[-1]] = g[PAIRS[-1]] - g[(ITERS - 2, ITERS - 1)]
        return solve_small(g)

    def sum_done(slot):
        all_others(red.at[slot], r_send.at[slot])

    def adjoint(v0, coef, x, z, r=0, size=None):
        rows = slice(HY + r, HY + r + (size or ry))
        out = coef[0] * v0[x + HX, z, rows]
        for k in range(1, ITERS):
            out = out + coef[k] * v[k - 1, x + HX, z, rows]
        return out

    def weights(s):
        width = m * ry
        yy = (t * ry + lax.broadcasted_iota(jnp.int32, (ry, 128), 0)).astype(jnp.float32)
        xx = (d * rx + lax.broadcasted_iota(jnp.int32, (ry, 128), 1)).astype(jnp.float32)
        two = 2.0 * spot_radius * spot_radius
        surface = jnp.zeros((ry, 128), jnp.float32)
        for k in range(path.shape[1]):
            cell = path[s, k]
            dx = xx - lax.div(cell, jnp.int32(width)).astype(jnp.float32)
            dy = yy - lax.rem(cell, jnp.int32(width)).astype(jnp.float32)
            surface = surface + jnp.exp(-dx * dx / two) * jnp.exp(-dy * dy / two)
        zz = lax.broadcasted_iota(jnp.int32, (1, rz), 1).astype(jnp.float32)
        fall = spot_peak * jnp.exp(-zz / decay_depth)
        lane = lax.broadcasted_iota(jnp.int32, (ry, 128), 1)

        def body(x, _):
            column = jnp.sum(jnp.where(lane == x, surface, 0.0), axis=1, keepdims=True)
            wgt[s, x] = lookup(melt[s, x], ABSORBS) * (1.0 + column * fall)
            return 0

        lax.fori_loop(0, rx, body, 0)

    halo_start(e1.at[0], 0)
    step = spread(0)
    loaded(1, 2)
    diagonals(1, e1.at[1])
    halo_start(e1.at[1], 3)
    step = spread(step)
    loaded(4, 5)
    diagonals(0, ec0)
    step = spread(step)
    loaded(3)
    factors(1)
    loaded(7)
    factors(0)
    while step < waves:
        step = spread(step)
    spread(step)
    powers_inside(e1.at[0], e1.at[1])
    halo_wait(e1.at[0], 0)
    halo_wait(e1.at[1], 3)
    powers_around(e1.at[0], e1.at[1])
    dots(e1.at[0], e1.at[1], 0)
    sum_start(0)
    loaded(6)
    halo_start(er0, 2, BACK)
    halo_start(ec0, 1)
    weights(1)
    weights(0)
    coef = sum_end(0)

    tail = ITERS - 1
    body = rx - tail
    PIECES = ((body, tail, 0, ry), (0, body, 0, ITERS), (0, body, ry - tail, tail), (0, body, ITERS, ry - tail - ITERS))

    def carry_copy(c):
        x, xs, y, ys = PIECES[c]
        piece = (pl.ds(x, xs), slice(None), pl.ds(y, ys))
        return pltpu.make_async_remote_copy(
            src_ref=cs.at[piece], dst_ref=cr.at[piece], send_sem=c_send.at[c], recv_sem=c_recv.at[c],
            device_id=(d + 1, t), device_id_type=MESH)

    def carry_start(*which):
        @pl.when(d < n - 1)
        def _():
            for c in which:
                carry_copy(c).start()

    def carry_make(start, stop, rows):
        def plane(x, _):
            for z in range(nz):
                for r, size in rows:
                    cs[x, z, r:r + size] = fac[1, x, r:r + size, zs(z)] * adjoint(e1.at[0], coef, x, z, r, size)
            return 0

        lax.fori_loop(start, stop, plane, 0)

    def rhs_make(*which):
        @pl.when(d > 0)
        def _():
            for c in which:
                carry_copy(c).wait_recv()
            start, count = PIECES[which[0]][:2]

            def plane(x, _):
                for c in which:
                    _, _, y, ys = PIECES[c]
                    for z in range(nz):
                        here = (x + HX, z, slice(HY + y, HY + y + ys))
                        er0[here] = er0[here] + cr[x, z, y:y + ys]
                return 0

            lax.fori_loop(start, start + count, plane, 0)

    carry_make(body, rx, ((0, ry),))
    carry_start(0)
    carry_make(0, body, ((0, 8), (ry - 8, 8)))
    carry_start(1, 2)
    carry_make(0, body, ((8, ry - 16),))
    carry_start(3)
    halo_done(er0, 2, BACK)
    halo_wait(er0, 2, BACK)

    @pl.when(d < n - 1)
    def _():
        for x in range(ITERS):
            for z in range(nz):
                here = (HX + rx + x, z, slice(HY, HY + ry))
                er0[here] = er0[here] + cs[x, z]

    rhs_make(0)
    halo_start(er0, 2, AHEAD)
    rhs_make(1, 2)
    halo_start(er0, 2, ASIDE)

    def late(x, _):
        for z in range(nz):
            ps_late[x, :, zs(z)] = wgt[1, x, :, zs(z)] * adjoint(e1.at[0], coef, x, z)
        return 0

    lax.fori_loop(0, rx, late, 0)
    rhs_make(3)
    powers_inside(er0, ec0)
    halo_wait(ec0, 1)
    halo_wait(er0, 2, AHEAD + ASIDE)
    powers_around(er0, ec0)
    dots(er0, ec0, 1)
    sum_start(1)
    halo_done(e1.at[0], 0)
    halo_done(e1.at[1], 3)
    halo_done(ec0, 1)
    halo_done(er0, 2, AHEAD + ASIDE)
    sum_done(0)

    @pl.when(d < n - 1)
    def _():
        for c in range(len(PIECES)):
            carry_copy(c).wait_send()

    coef0 = sum_end(1)
    for k in range(ITERS):
        weights_out[k] = jnp.broadcast_to(coef0[k], (8, LANES))
    sum_done(1)


def finish(ps_late, e, v, fac, wgt, coef, out_ps, out_carry, ps, carry, sems):
    rx, ry, rz = ps.shape
    nz = rz // LANES
    late = pltpu.make_async_copy(ps_late, out_ps.at[1], sems.at[0])
    late.start()
    part = max(1, rx // WRITES)
    c = [coef[k] for k in range(ITERS)]
    copies = [late]
    for q, low in enumerate(range(0, rx, part)):
        size = min(part, rx - low)

        def plane(x, _):
            for z in range(nz):
                lanes = slice(z * LANES, (z + 1) * LANES)
                for r in range(0, ry, 8):
                    rows = slice(HY + r, HY + r + 8)
                    a = c[0] * e[x + HX, z, rows]
                    for k in range(1, ITERS):
                        a = a + c[k] * v[k - 1, x + HX, z, rows]
                    ps[x, r:r + 8, lanes] = wgt[0, x, r:r + 8, lanes] * a
                    carry[x, r:r + 8, lanes] = fac[0, x, r:r + 8, lanes] * a
            return 0

        lax.fori_loop(low, low + size, plane, 0)
        piece = pl.ds(low, size)
        copies.append(pltpu.make_async_copy(ps.at[piece], out_ps.at[0, piece], sems.at[1 + 2 * q]))
        copies.append(pltpu.make_async_copy(carry.at[piece], out_carry.at[piece], sems.at[2 + 2 * q]))
        copies[-2].start()
        copies[-1].start()
    for copy in copies:
        copy.wait()


def per_device(n, m, temp_before, temp_after, melt_phase, objective_grad, laser_path):
    steps, rx, ry, rz = temp_before.shape
    ex, ey = rx + 2 * HX, ry + 2 * HY
    nz = rz // LANES
    waves = (max(n, m) - 2).bit_length()
    f32 = jnp.float32
    vm = pl.BlockSpec(memory_space=pltpu.VMEM)
    dma = pltpu.SemaphoreType.DMA
    results = pl.pallas_call(
        functools.partial(kernel, n, m),
        out_shape=tuple(
            pltpu.VMEM(shape, f32)
            for shape in (
                (rx, ry, rz),
                (ex, nz, ey, LANES),
                (ITERS - 1, ex, nz, ey, LANES),
                (steps, rx, ry, rz),
                (steps, rx, ry, rz),
                (ITERS, 8, LANES),
            )
        ),
        in_specs=[pl.BlockSpec(memory_space=pl.ANY)] * 4 + [pl.BlockSpec(memory_space=pltpu.SMEM)],
        out_specs=(vm,) * 6,
        scratch_shapes=[
            pltpu.VMEM((2, rx, ry, rz), f32),
            pltpu.VMEM((2, rx, ry, rz), f32),
            pltpu.VMEM((2, rx, ry, rz), jnp.int32),
            pltpu.VMEM((2, ex, nz, ey, LANES), f32),
            pltpu.VMEM((ex, nz, ey, LANES), f32),
            pltpu.VMEM((rx, nz, ry, LANES), f32),
            pltpu.VMEM((rx, nz, ry, LANES), f32),
            pltpu.VMEM((2, 8, LANES), f32),
            pltpu.VMEM((2, n * m, LANES), f32),
            dma((8 + 2 * nz,)),
            dma((4, 8)), dma((4, 8)),
            dma((4,)), dma((4,)),
            dma((2,)), dma((2,)),
            pltpu.SemaphoreType.REGULAR((waves,)),
        ],
        compiler_params=pltpu.CompilerParams(
            collective_id=0, has_side_effects=True, vmem_limit_bytes=56 * 1024 * 1024
        ),
    )(temp_before, temp_after, melt_phase, objective_grad, laser_path)
    hbm = pl.BlockSpec(memory_space=pl.ANY)
    parts = -(-rx // max(1, rx // WRITES))
    return pl.pallas_call(
        finish,
        out_shape=(
            jax.ShapeDtypeStruct((steps, rx, ry, rz), f32),
            jax.ShapeDtypeStruct((rx, ry, rz), f32),
        ),
        in_specs=[vm] * 6,
        out_specs=(hbm, hbm),
        scratch_shapes=[pltpu.VMEM((rx, ry, rz), f32), pltpu.VMEM((rx, ry, rz), f32), dma((1 + 2 * parts,))],
        compiler_params=pltpu.CompilerParams(vmem_limit_bytes=4 * 1024 * 1024),
    )(*results)


def solution(mesh):
    spec = P(None, "scan", "track", None)
    return jax.shard_map(
        functools.partial(per_device, mesh.shape["scan"], mesh.shape["track"]),
        mesh=mesh,
        in_specs=(spec, spec, spec, spec, P()),
        out_specs=(spec, P("scan", "track", None)),
        check_vma=False,
    )
```

```python
import functools

import jax
import jax.numpy as jnp
from jax import lax
from jax.experimental import pallas as pl
from jax.experimental.pallas import tpu as pltpu
from jax.sharding import PartitionSpec as P

ITERS = 4
CAPS = (0.6, 2.0, 0.9)
ABSORBS = (0.35, 0.5, 0.65)
spot_radius = 3.0
decay_depth = 4.0
spot_peak = 4.0

SHIFT = 7.25
SCALE = 3.0

HX = 4
HY = 8

DIRS = ((-1, 0), (1, 0), (-1, -1), (-1, 1), (1, -1), (1, 1), (0, -1), (0, 1))
BACK = ((-1, 0),)
AHEAD = ((1, -1), (1, 0), (1, 1))
ASIDE = ((0, -1), (0, 1))
PAIRS = tuple((i, j) for i in range(ITERS) for j in range(i, ITERS)) + ((ITERS - 1, ITERS),)
MESH = pl.DeviceIdType.MESH
LANES = 128
TRIPS = 2
DOT_TRIPS = 2
WRITES = 4


def lookup(melt, values):
    return jnp.where(
        melt == 0,
        jnp.float32(values[0]),
        jnp.where(melt == 1, jnp.float32(values[1]), jnp.float32(values[2])),
    )


def solve_small(g):
    def gram(i, j):
        return g[(min(i, j), max(i, j))]

    n = ITERS
    h = {}
    for i in range(n):
        for j in range(i, n):
            value = SCALE * gram(i + 1, j) + SHIFT * gram(i, j)
            if i > 0:
                value = value + SCALE * gram(i - 1, j)
            h[(i, j)] = value
    low, inv, y = {}, {}, {}
    for j in range(n):
        d = h[(j, j)]
        for k in range(j):
            d = d - low[(j, k)] * low[(j, k)] * inv[("d", k)]
        good = d > 1e-7 * h[(j, j)]
        inv[("d", j)] = jnp.where(good, d, 0.0)
        inv[j] = jnp.where(good, 1.0 / jnp.where(good, d, 1.0), 0.0)
        for i in range(j + 1, n):
            t = h[(j, i)]
            for k in range(j):
                t = t - low[(i, k)] * low[(j, k)] * inv[("d", k)]
            low[(i, j)] = t * inv[j]
    for i in range(n):
        t = gram(0, i)
        for k in range(i):
            t = t - low[(i, k)] * y[k]
        y[i] = t
    a = [None] * n
    for i in reversed(range(n)):
        t = y[i] * inv[i]
        for k in range(i + 1, n):
            t = t - low[(k, i)] * a[k]
        a[i] = t
    return a


def kernel(n, m, tb_in, ta_in, melt_in, grad_in, path, ps_late, er0, v, fac, wgt, weights_out,
           tb, ta, melt, e1, ec0, cs, cr, part, red,
           load_sem, h_send, h_recv, c_send, c_recv, r_send, r_recv, known):
    rx, ry, rz = tb.shape[1:]
    ex, ey = rx + 2 * HX, ry + 2 * HY
    nz = rz // LANES
    d = lax.axis_index("scan")
    t = lax.axis_index("track")

    def exists(dx, dy):
        ok = None
        if dx < 0:
            ok = d > 0
        if dx > 0:
            ok = d < n - 1
        if dy != 0:
            oky = (t > 0) if dy < 0 else (t < m - 1)
            ok = oky if ok is None else jnp.logical_and(ok, oky)
        return ok

    def at_distance(r):
        for dx, dy in DIRS:
            ok = None
            if dx != 0:
                ok = (d >= r) if dx < 0 else (d < n - r)
            if dy != 0:
                oky = (t >= r) if dy < 0 else (t < m - r)
                ok = oky if ok is None else jnp.logical_and(ok, oky)
            if (dx == 0 or r < n) and (dy == 0 or r < m):
                yield ok, (d + dx * r, t + dy * r)

    def greet(sem, r):
        for ok, device in at_distance(r):
            @pl.when(ok)
            def _(device=device):
                pl.semaphore_signal(sem, inc=1, device_id=device, device_id_type=MESH)

    def greeted(sem, r):
        count = jnp.int32(0)
        for ok, _ in at_distance(r):
            count = count + ok.astype(jnp.int32)
        pl.semaphore_wait(sem, count)

    barrier = pltpu.get_barrier_semaphore()
    greet(barrier, 1)

    def zero_halo(ref):
        @pl.when(d == 0)
        def _():
            ref[0:HX] = jnp.zeros((HX, nz, ey, LANES), jnp.float32)

        @pl.when(d == n - 1)
        def _():
            ref[ex - HX:ex] = jnp.zeros((HX, nz, ey, LANES), jnp.float32)

        @pl.when(t == 0)
        def _():
            ref[:, :, 0:HY] = jnp.zeros((ex, nz, HY, LANES), jnp.float32)

        @pl.when(t == m - 1)
        def _():
            ref[:, :, ey - HY:ey] = jnp.zeros((ex, nz, HY, LANES), jnp.float32)

    def zs(z):
        return slice(z * LANES, (z + 1) * LANES)

    loads = []
    for q, (s, kind) in enumerate([(1, 2), (1, 0), (1, 1), (1, 3), (0, 0), (0, 1), (0, 2), (0, 3)]):
        if kind == 2:
            where = e1.at[0] if s == 1 else er0
            parts = [
                pltpu.make_async_copy(
                    grad_in.at[s, :, :, pl.ds(z * LANES, LANES)],
                    where.at[pl.ds(HX, rx), z, pl.ds(HY, ry)],
                    load_sem.at[8 + s * nz + z],
                )
                for z in range(nz)
            ]
        else:
            src, dst = ((tb_in, tb), (melt_in, melt), None, (ta_in, ta))[kind]
            parts = [pltpu.make_async_copy(src.at[s], dst.at[s], load_sem.at[q])]
        loads.append(parts)

    def loaded(*which):
        for q in which:
            for c in loads[q]:
                c.wait()

    for c in loads[0]:
        c.start()
    zero_halo(e1.at[0])
    zero_halo(er0)

    def terms(s, x):
        base = lookup(melt[s, x], CAPS)
        h = jnp.tanh(tb[s, x])
        return base * (1.0 + 0.5 * h), base, h

    def diagonals(s, cap_ref):
        def body(x, _):
            cap, _, _ = terms(s, x)
            cap = (cap + (6.0 - SHIFT)) * (1.0 / SCALE)
            for z in range(nz):
                cap_ref[x + HX, z, HY:HY + ry] = cap[:, zs(z)]
            return 0

        lax.fori_loop(0, rx, body, 0)

    def factors(s):
        def body(x, _):
            cap, base, h = terms(s, x)
            slope = base * 0.5 * (1.0 - h * h)
            fac[s, x] = cap - slope * (ta[s, x] - tb[s, x])
            return 0

        lax.fori_loop(0, rx, body, 0)

    waves = known.shape[0]

    def spread(step):
        if 0 < step <= waves:
            greeted(known.at[step - 1], 2 ** (step - 1))
        if step < waves:
            greet(known.at[step], 2 ** step)
        return step + 1

    loaded(0)
    for parts in loads[1:]:
        for c in parts:
            c.start()
    greeted(barrier, 1)

    def span(delta, low, count, width):
        if delta == 0:
            return low, low, count
        if delta > 0:
            return low + count - width, low - width, width
        return low, low + count, width

    def halo_copy(ref, which, q):
        dx, dy = DIRS[q]
        wide = ITERS if which in (0, 2) else ITERS - 1
        if dx != 0 and dy != 0:
            wx = wy = wide - 2 if dx > 0 and dy > 0 else wide - 1
        else:
            wx = wide - 1 if dx > 0 else wide
            wy = wide - 1 if dy > 0 else wide
        x_src, x_dst, x_size = span(dx, HX, rx, wx)
        y_src, y_dst, y_size = span(dy, HY, ry, wy)
        if which == 2 and dx == 0:
            x_size = rx + ITERS - 1
        return pltpu.make_async_remote_copy(
            src_ref=ref.at[pl.ds(x_src, x_size), slice(None), pl.ds(y_src, y_size)],
            dst_ref=ref.at[pl.ds(x_dst, x_size), slice(None), pl.ds(y_dst, y_size)],
            send_sem=h_send.at[which, q],
            recv_sem=h_recv.at[which, q],
            device_id=(d + dx, t + dy),
            device_id_type=MESH,
        )

    def halo_start(ref, which, wanted=DIRS):
        for q, (dx, dy) in enumerate(DIRS):
            if (dx, dy) in wanted:
                @pl.when(exists(dx, dy))
                def _(q=q):
                    halo_copy(ref, which, q).start()

    def halo_wait(ref, which, wanted=DIRS):
        for q, (dx, dy) in enumerate(DIRS):
            if (dx, dy) in wanted:
                @pl.when(exists(-dx, -dy))
                def _(q=q):
                    halo_copy(ref, which, q).wait_recv()

    def halo_done(ref, which, wanted=DIRS):
        for q, (dx, dy) in enumerate(DIRS):
            if (dx, dy) in wanted:
                @pl.when(exists(dx, dy))
                def _(q=q):
                    halo_copy(ref, which, q).wait_send()

    lane8 = lax.broadcasted_iota(jnp.int32, (8, LANES), 1)
    first, final = lane8 == 0, lane8 == LANES - 1

    def advance(v0, cap_ref, k, start, count, tiles):
        at = [v0] + [v.at[q] for q in range(ITERS - 1)]
        trips = TRIPS if count % TRIPS == 0 and count * len(tiles) > 36 else 1
        planes = count // trips

        def trip(p, _):
            x = start + planes * p
            for r in tiles:
                c = [[at[k][x + q, z, r:r + 8] for z in range(nz)] for q in range(-1, planes + 1)]
                for q in range(planes):
                    mid = c[q + 1]
                    up = [pltpu.roll(w, 1, 1) for w in mid]
                    down = [pltpu.roll(w, LANES - 1, 1) for w in mid]
                    for z in range(nz):
                        above = jnp.where(first, up[z - 1] if z > 0 else 0.0, up[z])
                        below = jnp.where(final, down[z + 1] if z < nz - 1 else 0.0, down[z])
                        beside = (c[q][z] + c[q + 2][z]) + (above + below)
                        beside = beside + (at[k][x + q, z, r - 1:r + 7] + at[k][x + q, z, r + 1:r + 9])
                        new = cap_ref[x + q, z, r:r + 8] * mid[z] - beside * (1.0 / SCALE)
                        if k > 0:
                            new = new - at[k - 1][x + q, z, r:r + 8]
                        at[k + 1][x + q, z, r:r + 8] = new
            return 0

        if trips == 1:
            trip(0, 0)
        else:
            lax.fori_loop(0, trips, trip, 0)

    def inner_part(k):
        low, high = HY + 4 + k, HY + ry - 4 - k
        return low, high, [min(r, high - 8) for r in range(low, high, 8)]

    def powers_inside(v0, cap_ref):
        for k in range(ITERS - 1):
            advance(v0, cap_ref, k, HX + 1 + k, rx - 2 - 2 * k, inner_part(k)[2])

    def powers_around(v0, cap_ref):
        for k in range(ITERS - 1):
            low, high, tiles = inner_part(k)
            edge = [low - 8, high]
            first_plane = HX - (ITERS - 2) + k
            advance(v0, cap_ref, k, first_plane, HX + 1 + k - first_plane, edge[:1] + tiles + edge[1:])
            advance(v0, cap_ref, k, HX + rx - 1 - k, ITERS, edge[:1] + tiles + edge[1:])
            advance(v0, cap_ref, k, HX + 1 + k, rx - 2 - 2 * k, edge)
            zero_halo(v.at[k])

    def dots(v0, cap_ref, slot):
        at = [v0] + [v.at[k] for k in range(ITERS - 1)]
        group = max(1, rx // DOT_TRIPS)

        def body(p, acc):
            acc = list(acc)
            for g in range(group):
                x = HX + p * group + g
                for r in range(HY, HY + ry, 8):
                    tips = [at[-1][x, z, r:r + 8] for z in range(nz)]
                    for z in range(nz):
                        vals = [ref[x, z, r:r + 8] for ref in at[:-1]] + [tips[z]]
                        over = tips[z + 1] if z < nz - 1 else 0.0
                        below = pltpu.roll(jnp.where(first, over, tips[z]), LANES - 1, 1)
                        after = at[-1][x + 1, z, r:r + 8] + at[-1][x, z, r + 1:r + 9] + below
                        vals.append(cap_ref[x, z, r:r + 8] * tips[z] - after * (2.0 / SCALE))
                        for q, (i, j) in enumerate(PAIRS):
                            acc[q] = acc[q] + vals[i] * vals[j]
            return tuple(acc)

        acc = lax.fori_loop(0, rx // group, body, tuple(jnp.zeros((8, LANES), jnp.float32) for _ in PAIRS))
        lane = lax.broadcasted_iota(jnp.int32, (1, LANES), 1)
        row = jnp.zeros((1, LANES), jnp.float32)
        for q, a in enumerate(acc):
            s = jnp.sum(jnp.sum(a, axis=0, keepdims=True), axis=1, keepdims=True)
            row = jnp.where(lane == q, s, row)
        part[slot, 0:1] = row

    me = d * m + t
    others = n * m - 1

    def sum_copy(slot, device):
        return pltpu.make_async_remote_copy(
            src_ref=part.at[slot, pl.ds(0, 1)],
            dst_ref=red.at[slot, pl.ds(me, 1)],
            send_sem=r_send.at[slot],
            recv_sem=r_recv.at[slot],
            device_id=device,
            device_id_type=MESH,
        )

    def sum_start(slot):
        for j in range(m):
            row = jnp.where(2 * t < m, m - 1 - j, j)
            for k in range(n):
                column = lax.rem(d + (n // 2 + k) % n, n)
                if (n // 2 + k) % n == 0:
                    @pl.when(row != t)
                    def _(row=row):
                        sum_copy(slot, (d, row)).start()
                else:
                    sum_copy(slot, (column, row)).start()
        red[slot, pl.ds(me, 1)] = part[slot, 0:1]

    def all_others(ref, sem):
        view = ref.at[pl.ds(0, others)]
        pltpu.make_async_copy(view, view, sem).wait()

    def sum_end(slot):
        all_others(red.at[slot], r_recv.at[slot])
        total = jnp.sum(red[slot], axis=0, keepdims=True)
        lane = lax.broadcasted_iota(jnp.int32, (1, LANES), 1)
        g = {}
        for q, pair in enumerate(PAIRS):
            g[pair] = jnp.sum(jnp.where(lane == q, total, 0.0), axis=1, keepdims=True)
        g[PAIRS[-1]] = g[PAIRS[-1]] - g[(ITERS - 2, ITERS - 1)]
        return solve_small(g)

    def sum_done(slot):
        all_others(red.at[slot], r_send.at[slot])

    def adjoint(v0, coef, x, z, r=0, size=None):
        rows = slice(HY + r, HY + r + (size or ry))
        out = coef[0] * v0[x + HX, z, rows]
        for k in range(1, ITERS):
            out = out + coef[k] * v[k - 1, x + HX, z, rows]
        return out

    def weights(s):
        width = m * ry
        yy = (t * ry + lax.broadcasted_iota(jnp.int32, (ry, 128), 0)).astype(jnp.float32)
        xx = (d * rx + lax.broadcasted_iota(jnp.int32, (ry, 128), 1)).astype(jnp.float32)
        two = 2.0 * spot_radius * spot_radius
        surface = jnp.zeros((ry, 128), jnp.float32)
        for k in range(path.shape[1]):
            cell = path[s, k]
            dx = xx - lax.div(cell, jnp.int32(width)).astype(jnp.float32)
            dy = yy - lax.rem(cell, jnp.int32(width)).astype(jnp.float32)
            surface = surface + jnp.exp(-dx * dx / two) * jnp.exp(-dy * dy / two)
        zz = lax.broadcasted_iota(jnp.int32, (1, rz), 1).astype(jnp.float32)
        fall = spot_peak * jnp.exp(-zz / decay_depth)
        lane = lax.broadcasted_iota(jnp.int32, (ry, 128), 1)

        def body(x, _):
            column = jnp.sum(jnp.where(lane == x, surface, 0.0), axis=1, keepdims=True)
            wgt[s, x] = lookup(melt[s, x], ABSORBS) * (1.0 + column * fall)
            return 0

        lax.fori_loop(0, rx, body, 0)

    halo_start(e1.at[0], 0)
    step = spread(0)
    loaded(1, 2)
    diagonals(1, e1.at[1])
    halo_start(e1.at[1], 3)
    step = spread(step)
    loaded(4, 5)
    diagonals(0, ec0)
    step = spread(step)
    loaded(3)
    factors(1)
    loaded(7)
    factors(0)
    while step < waves:
        step = spread(step)
    spread(step)
    powers_inside(e1.at[0], e1.at[1])
    halo_wait(e1.at[0], 0)
    halo_wait(e1.at[1], 3)
    powers_around(e1.at[0], e1.at[1])
    dots(e1.at[0], e1.at[1], 0)
    sum_start(0)
    loaded(6)
    halo_start(er0, 2, BACK)
    halo_start(ec0, 1)
    weights(1)
    weights(0)
    coef = sum_end(0)

    tail = ITERS - 1
    body = rx - tail
    PIECES = ((body, tail, 0, ry), (0, body, 0, ITERS), (0, body, ry - tail, tail), (0, body, ITERS, ry - tail - ITERS))

    def carry_copy(c):
        x, xs, y, ys = PIECES[c]
        piece = (pl.ds(x, xs), slice(None), pl.ds(y, ys))
        return pltpu.make_async_remote_copy(
            src_ref=cs.at[piece], dst_ref=cr.at[piece], send_sem=c_send.at[c], recv_sem=c_recv.at[c],
            device_id=(d + 1, t), device_id_type=MESH)

    def carry_start(*which):
        @pl.when(d < n - 1)
        def _():
            for c in which:
                carry_copy(c).start()

    def carry_make(start, stop, rows):
        def plane(x, _):
            for z in range(nz):
                for r, size in rows:
                    cs[x, z, r:r + size] = fac[1, x, r:r + size, zs(z)] * adjoint(e1.at[0], coef, x, z, r, size)
            return 0

        lax.fori_loop(start, stop, plane, 0)

    def rhs_make(*which):
        @pl.when(d > 0)
        def _():
            for c in which:
                carry_copy(c).wait_recv()
            start, count = PIECES[which[0]][:2]

            def plane(x, _):
                for c in which:
                    _, _, y, ys = PIECES[c]
                    for z in range(nz):
                        here = (x + HX, z, slice(HY + y, HY + y + ys))
                        er0[here] = er0[here] + cr[x, z, y:y + ys]
                return 0

            lax.fori_loop(start, start + count, plane, 0)

    carry_make(body, rx, ((0, ry),))
    carry_start(0)
    carry_make(0, body, ((0, 8), (ry - 8, 8)))
    carry_start(1, 2)
    carry_make(0, body, ((8, ry - 16),))
    carry_start(3)
    halo_done(er0, 2, BACK)
    halo_wait(er0, 2, BACK)

    @pl.when(d < n - 1)
    def _():
        for x in range(ITERS):
            for z in range(nz):
                here = (HX + rx + x, z, slice(HY, HY + ry))
                er0[here] = er0[here] + cs[x, z]

    rhs_make(0)
    halo_start(er0, 2, AHEAD)
    rhs_make(1, 2)
    halo_start(er0, 2, ASIDE)

    def late(x, _):
        for z in range(nz):
            ps_late[x, :, zs(z)] = wgt[1, x, :, zs(z)] * adjoint(e1.at[0], coef, x, z)
        return 0

    lax.fori_loop(0, rx, late, 0)
    rhs_make(3)
    powers_inside(er0, ec0)
    halo_wait(ec0, 1)
    halo_wait(er0, 2, AHEAD + ASIDE)
    powers_around(er0, ec0)
    dots(er0, ec0, 1)
    sum_start(1)
    halo_done(e1.at[0], 0)
    halo_done(e1.at[1], 3)
    halo_done(ec0, 1)
    halo_done(er0, 2, AHEAD + ASIDE)
    sum_done(0)

    @pl.when(d < n - 1)
    def _():
        for c in range(len(PIECES)):
            carry_copy(c).wait_send()

    coef0 = sum_end(1)
    for k in range(ITERS):
        weights_out[k] = jnp.broadcast_to(coef0[k], (8, LANES))
    sum_done(1)


def finish(ps_late, e, v, fac, wgt, coef, out_ps, out_carry, ps, carry, sems):
    rx, ry, rz = ps.shape
    nz = rz // LANES
    late = pltpu.make_async_copy(ps_late, out_ps.at[1], sems.at[0])
    late.start()
    part = max(1, rx // WRITES)
    c = [coef[k] for k in range(ITERS)]
    copies = [late]
    for q, low in enumerate(range(0, rx, part)):
        size = min(part, rx - low)

        def plane(x, _):
            for z in range(nz):
                lanes = slice(z * LANES, (z + 1) * LANES)
                for r in range(0, ry, 8):
                    rows = slice(HY + r, HY + r + 8)
                    a = c[0] * e[x + HX, z, rows]
                    for k in range(1, ITERS):
                        a = a + c[k] * v[k - 1, x + HX, z, rows]
                    ps[x, r:r + 8, lanes] = wgt[0, x, r:r + 8, lanes] * a
                    carry[x, r:r + 8, lanes] = fac[0, x, r:r + 8, lanes] * a
            return 0

        lax.fori_loop(low, low + size, plane, 0)
        piece = pl.ds(low, size)
        copies.append(pltpu.make_async_copy(ps.at[piece], out_ps.at[0, piece], sems.at[1 + 2 * q]))
        copies.append(pltpu.make_async_copy(carry.at[piece], out_carry.at[piece], sems.at[2 + 2 * q]))
        copies[-2].start()
        copies[-1].start()
    for copy in copies:
        copy.wait()


def per_device(n, m, temp_before, temp_after, melt_phase, objective_grad, laser_path):
    steps, rx, ry, rz = temp_before.shape
    ex, ey = rx + 2 * HX, ry + 2 * HY
    nz = rz // LANES
    waves = (max(n, m) - 2).bit_length()
    f32 = jnp.float32
    vm = pl.BlockSpec(memory_space=pltpu.VMEM)
    dma = pltpu.SemaphoreType.DMA
    results = pl.pallas_call(
        functools.partial(kernel, n, m),
        out_shape=tuple(
            pltpu.VMEM(shape, f32)
            for shape in (
                (rx, ry, rz),
                (ex, nz, ey, LANES),
                (ITERS - 1, ex, nz, ey, LANES),
                (steps, rx, ry, rz),
                (steps, rx, ry, rz),
                (ITERS, 8, LANES),
            )
        ),
        in_specs=[pl.BlockSpec(memory_space=pl.ANY)] * 4 + [pl.BlockSpec(memory_space=pltpu.SMEM)],
        out_specs=(vm,) * 6,
        scratch_shapes=[
            pltpu.VMEM((2, rx, ry, rz), f32),
            pltpu.VMEM((2, rx, ry, rz), f32),
            pltpu.VMEM((2, rx, ry, rz), jnp.int32),
            pltpu.VMEM((2, ex, nz, ey, LANES), f32),
            pltpu.VMEM((ex, nz, ey, LANES), f32),
            pltpu.VMEM((rx, nz, ry, LANES), f32),
            pltpu.VMEM((rx, nz, ry, LANES), f32),
            pltpu.VMEM((2, 8, LANES), f32),
            pltpu.VMEM((2, n * m, LANES), f32),
            dma((8 + 2 * nz,)),
            dma((4, 8)), dma((4, 8)),
            dma((4,)), dma((4,)),
            dma((2,)), dma((2,)),
            pltpu.SemaphoreType.REGULAR((waves,)),
        ],
        compiler_params=pltpu.CompilerParams(
            collective_id=0, has_side_effects=True, vmem_limit_bytes=56 * 1024 * 1024
        ),
    )(temp_before, temp_after, melt_phase, objective_grad, laser_path)
    hbm = pl.BlockSpec(memory_space=pl.ANY)
    parts = -(-rx // max(1, rx // WRITES))
    return pl.pallas_call(
        finish,
        out_shape=(
            jax.ShapeDtypeStruct((steps, rx, ry, rz), f32),
            jax.ShapeDtypeStruct((rx, ry, rz), f32),
        ),
        in_specs=[vm] * 6,
        out_specs=(hbm, hbm),
        scratch_shapes=[pltpu.VMEM((rx, ry, rz), f32), pltpu.VMEM((rx, ry, rz), f32), dma((1 + 2 * parts,))],
        compiler_params=pltpu.CompilerParams(vmem_limit_bytes=4 * 1024 * 1024),
    )(*results)


def solution(mesh):
    spec = P(None, "scan", "track", None)
    return jax.shard_map(
        functools.partial(per_device, mesh.shape["scan"], mesh.shape["track"]),
        mesh=mesh,
        in_specs=(spec, spec, spec, spec, P()),
        out_specs=(spec, P("scan", "track", None)),
        check_vma=False,
    )
```

```python
import functools

import jax
import jax.numpy as jnp
from jax import lax
from jax.experimental import pallas as pl
from jax.experimental.pallas import tpu as pltpu
from jax.sharding import PartitionSpec as P

ITERS = 4
CAPS = (0.6, 2.0, 0.9)
ABSORBS = (0.35, 0.5, 0.65)
spot_radius = 3.0
decay_depth = 4.0
spot_peak = 4.0

SHIFT = 7.25
SCALE = 3.0

HX = 4
HY = 8

DIRS = ((-1, 0), (1, 0), (-1, -1), (-1, 1), (1, -1), (1, 1), (0, -1), (0, 1))
BACK = ((-1, 0),)
AHEAD = ((1, -1), (1, 0), (1, 1))
ASIDE = ((0, -1), (0, 1))
PAIRS = tuple((i, j) for i in range(ITERS) for j in range(i, ITERS)) + ((ITERS - 1, ITERS),)
MESH = pl.DeviceIdType.MESH
LANES = 128
DIAG, CARRY, RHS, LAST = 4, 16, 16, 4
TRIPS = 2
DOT_TRIPS = 2
WRITES = 4


def lookup(melt, values):
    return jnp.where(
        melt == 0,
        jnp.float32(values[0]),
        jnp.where(melt == 1, jnp.float32(values[1]), jnp.float32(values[2])),
    )


def solve_small(g):
    def gram(i, j):
        return g[(min(i, j), max(i, j))]

    n = ITERS
    h = {}
    for i in range(n):
        for j in range(i, n):
            value = SCALE * gram(i + 1, j) + SHIFT * gram(i, j)
            if i > 0:
                value = value + SCALE * gram(i - 1, j)
            h[(i, j)] = value
    low, inv, y = {}, {}, {}
    for j in range(n):
        d = h[(j, j)]
        for k in range(j):
            d = d - low[(j, k)] * low[(j, k)] * inv[("d", k)]
        good = d > 1e-7 * h[(j, j)]
        inv[("d", j)] = jnp.where(good, d, 0.0)
        inv[j] = jnp.where(good, 1.0 / jnp.where(good, d, 1.0), 0.0)
        for i in range(j + 1, n):
            t = h[(j, i)]
            for k in range(j):
                t = t - low[(i, k)] * low[(j, k)] * inv[("d", k)]
            low[(i, j)] = t * inv[j]
    for i in range(n):
        t = gram(0, i)
        for k in range(i):
            t = t - low[(i, k)] * y[k]
        y[i] = t
    a = [None] * n
    for i in reversed(range(n)):
        t = y[i] * inv[i]
        for k in range(i + 1, n):
            t = t - low[(k, i)] * a[k]
        a[i] = t
    return a


def sweep(start, stop, group, body):
    trips = (stop - start) // group
    if trips > 1:
        def trip(p, _):
            for g in range(group):
                body(start + p * group + g, 0)
            return 0

        lax.fori_loop(0, trips, trip, 0)
        start += trips * group
    for x in range(start, stop):
        body(x, 0)


def kernel(n, m, tb_in, ta_in, melt_in, grad_in, path, ps_late, er0, v, fac, wgt, weights_out,
           tb, ta, melt, e1, ec0, cs, cr, part, red,
           load_sem, h_send, h_recv, c_send, c_recv, r_send, r_recv, known):
    rx, ry, rz = tb.shape[1:]
    ex, ey = rx + 2 * HX, ry + 2 * HY
    nz = rz // LANES
    d = lax.axis_index("scan")
    t = lax.axis_index("track")

    def exists(dx, dy):
        ok = None
        if dx < 0:
            ok = d > 0
        if dx > 0:
            ok = d < n - 1
        if dy != 0:
            oky = (t > 0) if dy < 0 else (t < m - 1)
            ok = oky if ok is None else jnp.logical_and(ok, oky)
        return ok

    def at_distance(r):
        for dx, dy in DIRS:
            ok = None
            if dx != 0:
                ok = (d >= r) if dx < 0 else (d < n - r)
            if dy != 0:
                oky = (t >= r) if dy < 0 else (t < m - r)
                ok = oky if ok is None else jnp.logical_and(ok, oky)
            if (dx == 0 or r < n) and (dy == 0 or r < m):
                yield ok, (d + dx * r, t + dy * r)

    def greet(sem, r):
        for ok, device in at_distance(r):
            @pl.when(ok)
            def _(device=device):
                pl.semaphore_signal(sem, inc=1, device_id=device, device_id_type=MESH)

    def greeted(sem, r):
        count = jnp.int32(0)
        for ok, _ in at_distance(r):
            count = count + ok.astype(jnp.int32)
        pl.semaphore_wait(sem, count)

    barrier = pltpu.get_barrier_semaphore()
    greet(barrier, 1)

    def zero_halo(ref):
        @pl.when(d == 0)
        def _():
            ref[0:HX] = jnp.zeros((HX, nz, ey, LANES), jnp.float32)

        @pl.when(d == n - 1)
        def _():
            ref[ex - HX:ex] = jnp.zeros((HX, nz, ey, LANES), jnp.float32)

        @pl.when(t == 0)
        def _():
            ref[:, :, 0:HY] = jnp.zeros((ex, nz, HY, LANES), jnp.float32)

        @pl.when(t == m - 1)
        def _():
            ref[:, :, ey - HY:ey] = jnp.zeros((ex, nz, HY, LANES), jnp.float32)

    def zs(z):
        return slice(z * LANES, (z + 1) * LANES)

    loads = []
    for q, (s, kind) in enumerate([(1, 2), (1, 0), (1, 1), (1, 3), (0, 0), (0, 1), (0, 2), (0, 3)]):
        if kind == 2:
            where = e1.at[0] if s == 1 else er0
            parts = [
                pltpu.make_async_copy(
                    grad_in.at[s, :, :, pl.ds(z * LANES, LANES)],
                    where.at[pl.ds(HX, rx), z, pl.ds(HY, ry)],
                    load_sem.at[8 + s * nz + z],
                )
                for z in range(nz)
            ]
        else:
            src, dst = ((tb_in, tb), (melt_in, melt), None, (ta_in, ta))[kind]
            parts = [pltpu.make_async_copy(src.at[s], dst.at[s], load_sem.at[q])]
        loads.append(parts)

    def loaded(*which):
        for q in which:
            for c in loads[q]:
                c.wait()

    for c in loads[0]:
        c.start()
    zero_halo(e1.at[0])
    zero_halo(er0)

    def terms(s, x):
        base = lookup(melt[s, x], CAPS)
        h = jnp.tanh(tb[s, x])
        return base * (1.0 + 0.5 * h), base, h

    def diagonals(s, cap_ref):
        def body(x, _):
            cap, _, _ = terms(s, x)
            cap = (cap + (6.0 - SHIFT)) * (1.0 / SCALE)
            for z in range(nz):
                cap_ref[x + HX, z, HY:HY + ry] = cap[:, zs(z)]
            return 0

        sweep(0, rx, DIAG, body)

    def factors(s):
        def body(x, _):
            cap, base, h = terms(s, x)
            slope = base * 0.5 * (1.0 - h * h)
            fac[s, x] = cap - slope * (ta[s, x] - tb[s, x])
            return 0

        lax.fori_loop(0, rx, body, 0)

    waves = known.shape[0]

    def spread(step):
        if 0 < step <= waves:
            greeted(known.at[step - 1], 2 ** (step - 1))
        if step < waves:
            greet(known.at[step], 2 ** step)
        return step + 1

    loaded(0)
    for parts in loads[1:]:
        for c in parts:
            c.start()
    greeted(barrier, 1)

    def span(delta, low, count, width):
        if delta == 0:
            return low, low, count
        if delta > 0:
            return low + count - width, low - width, width
        return low, low + count, width

    def halo_copy(ref, which, q):
        dx, dy = DIRS[q]
        wide = ITERS if which in (0, 2) else ITERS - 1
        if dx != 0 and dy != 0:
            wx = wy = wide - 2 if dx > 0 and dy > 0 else wide - 1
        else:
            wx = wide - 1 if dx > 0 else wide
            wy = wide - 1 if dy > 0 else wide
        x_src, x_dst, x_size = span(dx, HX, rx, wx)
        y_src, y_dst, y_size = span(dy, HY, ry, wy)
        if which == 2 and dx == 0:
            x_size = rx + ITERS - 1
        return pltpu.make_async_remote_copy(
            src_ref=ref.at[pl.ds(x_src, x_size), slice(None), pl.ds(y_src, y_size)],
            dst_ref=ref.at[pl.ds(x_dst, x_size), slice(None), pl.ds(y_dst, y_size)],
            send_sem=h_send.at[which, q],
            recv_sem=h_recv.at[which, q],
            device_id=(d + dx, t + dy),
            device_id_type=MESH,
        )

    def halo_start(ref, which, wanted=DIRS):
        for q, (dx, dy) in enumerate(DIRS):
            if (dx, dy) in wanted:
                @pl.when(exists(dx, dy))
                def _(q=q):
                    halo_copy(ref, which, q).start()

    def halo_wait(ref, which, wanted=DIRS):
        for q, (dx, dy) in enumerate(DIRS):
            if (dx, dy) in wanted:
                @pl.when(exists(-dx, -dy))
                def _(q=q):
                    halo_copy(ref, which, q).wait_recv()

    def halo_done(ref, which, wanted=DIRS):
        for q, (dx, dy) in enumerate(DIRS):
            if (dx, dy) in wanted:
                @pl.when(exists(dx, dy))
                def _(q=q):
                    halo_copy(ref, which, q).wait_send()

    lane8 = lax.broadcasted_iota(jnp.int32, (8, LANES), 1)
    first, final = lane8 == 0, lane8 == LANES - 1

    def advance(v0, cap_ref, k, start, count, tiles):
        at = [v0] + [v.at[q] for q in range(ITERS - 1)]
        trips = TRIPS if count % TRIPS == 0 and count * len(tiles) > 36 else 1
        planes = count // trips

        def trip(p, _):
            x = start + planes * p
            for r in tiles:
                c = [[at[k][x + q, z, r:r + 8] for z in range(nz)] for q in range(-1, planes + 1)]
                for q in range(planes):
                    mid = c[q + 1]
                    up = [pltpu.roll(w, 1, 1) for w in mid]
                    down = [pltpu.roll(w, LANES - 1, 1) for w in mid]
                    for z in range(nz):
                        above = jnp.where(first, up[z - 1] if z > 0 else 0.0, up[z])
                        below = jnp.where(final, down[z + 1] if z < nz - 1 else 0.0, down[z])
                        beside = (c[q][z] + c[q + 2][z]) + (above + below)
                        beside = beside + (at[k][x + q, z, r - 1:r + 7] + at[k][x + q, z, r + 1:r + 9])
                        new = cap_ref[x + q, z, r:r + 8] * mid[z] - beside * (1.0 / SCALE)
                        if k > 0:
                            new = new - at[k - 1][x + q, z, r:r + 8]
                        at[k + 1][x + q, z, r:r + 8] = new
            return 0

        if trips == 1:
            trip(0, 0)
        else:
            lax.fori_loop(0, trips, trip, 0)

    def inner_part(k):
        low, high = HY + 4 + k, HY + ry - 4 - k
        return low, high, [min(r, high - 8) for r in range(low, high, 8)]

    def powers_inside(v0, cap_ref):
        for k in range(ITERS - 1):
            advance(v0, cap_ref, k, HX + 1 + k, rx - 2 - 2 * k, inner_part(k)[2])

    def powers_around(v0, cap_ref):
        for k in range(ITERS - 1):
            low, high, tiles = inner_part(k)
            edge = [low - 8, high]
            first_plane = HX - (ITERS - 2) + k
            advance(v0, cap_ref, k, first_plane, HX + 1 + k - first_plane, edge[:1] + tiles + edge[1:])
            advance(v0, cap_ref, k, HX + rx - 1 - k, ITERS, edge[:1] + tiles + edge[1:])
            advance(v0, cap_ref, k, HX + 1 + k, rx - 2 - 2 * k, edge)
            zero_halo(v.at[k])

    def dots(v0, cap_ref, slot):
        at = [v0] + [v.at[k] for k in range(ITERS - 1)]
        group = max(1, rx // DOT_TRIPS)

        def body(p, acc):
            acc = list(acc)
            for g in range(group):
                x = HX + p * group + g
                for r in range(HY, HY + ry, 8):
                    tips = [at[-1][x, z, r:r + 8] for z in range(nz)]
                    for z in range(nz):
                        vals = [ref[x, z, r:r + 8] for ref in at[:-1]] + [tips[z]]
                        over = tips[z + 1] if z < nz - 1 else 0.0
                        below = pltpu.roll(jnp.where(first, over, tips[z]), LANES - 1, 1)
                        after = at[-1][x + 1, z, r:r + 8] + at[-1][x, z, r + 1:r + 9] + below
                        vals.append(cap_ref[x, z, r:r + 8] * tips[z] - after * (2.0 / SCALE))
                        for q, (i, j) in enumerate(PAIRS):
                            acc[q] = acc[q] + vals[i] * vals[j]
            return tuple(acc)

        acc = lax.fori_loop(0, rx // group, body, tuple(jnp.zeros((8, LANES), jnp.float32) for _ in PAIRS))
        lane = lax.broadcasted_iota(jnp.int32, (1, LANES), 1)
        row = jnp.zeros((1, LANES), jnp.float32)
        for q, a in enumerate(acc):
            s = jnp.sum(jnp.sum(a, axis=0, keepdims=True), axis=1, keepdims=True)
            row = jnp.where(lane == q, s, row)
        part[slot, 0:1] = row

    me = d * m + t
    others = n * m - 1

    def sum_copy(slot, device):
        return pltpu.make_async_remote_copy(
            src_ref=part.at[slot, pl.ds(0, 1)],
            dst_ref=red.at[slot, pl.ds(me, 1)],
            send_sem=r_send.at[slot],
            recv_sem=r_recv.at[slot],
            device_id=device,
            device_id_type=MESH,
        )

    def sum_start(slot):
        for j in range(m):
            row = jnp.where(2 * t < m, m - 1 - j, j)
            for k in range(n):
                column = lax.rem(d + (n // 2 + k) % n, n)
                if (n // 2 + k) % n == 0:
                    @pl.when(row != t)
                    def _(row=row):
                        sum_copy(slot, (d, row)).start()
                else:
                    sum_copy(slot, (column, row)).start()
        red[slot, pl.ds(me, 1)] = part[slot, 0:1]

    def all_others(ref, sem):
        view = ref.at[pl.ds(0, others)]
        pltpu.make_async_copy(view, view, sem).wait()

    def sum_end(slot):
        all_others(red.at[slot], r_recv.at[slot])
        total = jnp.sum(red[slot], axis=0, keepdims=True)
        lane = lax.broadcasted_iota(jnp.int32, (1, LANES), 1)
        g = {}
        for q, pair in enumerate(PAIRS):
            g[pair] = jnp.sum(jnp.where(lane == q, total, 0.0), axis=1, keepdims=True)
        g[PAIRS[-1]] = g[PAIRS[-1]] - g[(ITERS - 2, ITERS - 1)]
        return solve_small(g)

    def sum_done(slot):
        all_others(red.at[slot], r_send.at[slot])

    def adjoint(v0, coef, x, z, r=0, size=None):
        rows = slice(HY + r, HY + r + (size or ry))
        out = coef[0] * v0[x + HX, z, rows]
        for k in range(1, ITERS):
            out = out + coef[k] * v[k - 1, x + HX, z, rows]
        return out

    def weights(s):
        width = m * ry
        yy = (t * ry + lax.broadcasted_iota(jnp.int32, (ry, 128), 0)).astype(jnp.float32)
        xx = (d * rx + lax.broadcasted_iota(jnp.int32, (ry, 128), 1)).astype(jnp.float32)
        two = 2.0 * spot_radius * spot_radius
        surface = jnp.zeros((ry, 128), jnp.float32)
        for k in range(path.shape[1]):
            cell = path[s, k]
            dx = xx - lax.div(cell, jnp.int32(width)).astype(jnp.float32)
            dy = yy - lax.rem(cell, jnp.int32(width)).astype(jnp.float32)
            surface = surface + jnp.exp(-dx * dx / two) * jnp.exp(-dy * dy / two)
        zz = lax.broadcasted_iota(jnp.int32, (1, rz), 1).astype(jnp.float32)
        fall = spot_peak * jnp.exp(-zz / decay_depth)
        lane = lax.broadcasted_iota(jnp.int32, (ry, 128), 1)

        def body(x, _):
            column = jnp.sum(jnp.where(lane == x, surface, 0.0), axis=1, keepdims=True)
            wgt[s, x] = lookup(melt[s, x], ABSORBS) * (1.0 + column * fall)
            return 0

        lax.fori_loop(0, rx, body, 0)

    halo_start(e1.at[0], 0)
    step = spread(0)
    loaded(1, 2)
    diagonals(1, e1.at[1])
    halo_start(e1.at[1], 3)
    step = spread(step)
    loaded(4, 5)
    diagonals(0, ec0)
    step = spread(step)
    loaded(3)
    factors(1)
    loaded(7)
    factors(0)
    while step < waves:
        step = spread(step)
    spread(step)
    powers_inside(e1.at[0], e1.at[1])
    halo_wait(e1.at[0], 0)
    halo_wait(e1.at[1], 3)
    powers_around(e1.at[0], e1.at[1])
    dots(e1.at[0], e1.at[1], 0)
    sum_start(0)
    loaded(6)
    halo_start(er0, 2, BACK)
    halo_start(ec0, 1)
    weights(1)
    weights(0)
    coef = sum_end(0)

    tail = ITERS - 1
    body = rx - tail
    PIECES = ((body, tail, 0, ry), (0, body, 0, ITERS), (0, body, ry - tail, tail), (0, body, ITERS, ry - tail - ITERS))

    def carry_copy(c):
        x, xs, y, ys = PIECES[c]
        piece = (pl.ds(x, xs), slice(None), pl.ds(y, ys))
        return pltpu.make_async_remote_copy(
            src_ref=cs.at[piece], dst_ref=cr.at[piece], send_sem=c_send.at[c], recv_sem=c_recv.at[c],
            device_id=(d + 1, t), device_id_type=MESH)

    def carry_start(*which):
        @pl.when(d < n - 1)
        def _():
            for c in which:
                carry_copy(c).start()

    def carry_make(start, stop, rows):
        def plane(x, _):
            for z in range(nz):
                for r, size in rows:
                    cs[x, z, r:r + size] = fac[1, x, r:r + size, zs(z)] * adjoint(e1.at[0], coef, x, z, r, size)
            return 0

        sweep(start, stop, CARRY, plane)

    def rhs_make(*which):
        @pl.when(d > 0)
        def _():
            for c in which:
                carry_copy(c).wait_recv()
            start, count = PIECES[which[0]][:2]

            def plane(x, _):
                for c in which:
                    _, _, y, ys = PIECES[c]
                    for z in range(nz):
                        here = (x + HX, z, slice(HY + y, HY + y + ys))
                        er0[here] = er0[here] + cr[x, z, y:y + ys]
                return 0

            sweep(start, start + count, RHS, plane)

    carry_make(body, rx, ((0, ry),))
    carry_start(0)
    carry_make(0, body, ((0, 8), (ry - 8, 8)))
    carry_start(1, 2)
    carry_make(0, body, ((8, ry - 16),))
    carry_start(3)
    halo_done(er0, 2, BACK)
    halo_wait(er0, 2, BACK)

    @pl.when(d < n - 1)
    def _():
        for x in range(ITERS):
            for z in range(nz):
                here = (HX + rx + x, z, slice(HY, HY + ry))
                er0[here] = er0[here] + cs[x, z]

    rhs_make(0)
    halo_start(er0, 2, AHEAD)
    rhs_make(1, 2)
    halo_start(er0, 2, ASIDE)

    def late(x, _):
        for z in range(nz):
            ps_late[x, :, zs(z)] = wgt[1, x, :, zs(z)] * adjoint(e1.at[0], coef, x, z)
        return 0

    lax.fori_loop(0, rx, late, 0)
    rhs_make(3)
    powers_inside(er0, ec0)
    halo_wait(ec0, 1)
    halo_wait(er0, 2, AHEAD + ASIDE)
    powers_around(er0, ec0)
    dots(er0, ec0, 1)
    sum_start(1)
    halo_done(e1.at[0], 0)
    halo_done(e1.at[1], 3)
    halo_done(ec0, 1)
    halo_done(er0, 2, AHEAD + ASIDE)
    sum_done(0)

    @pl.when(d < n - 1)
    def _():
        for c in range(len(PIECES)):
            carry_copy(c).wait_send()

    coef0 = sum_end(1)
    for k in range(ITERS):
        weights_out[k] = jnp.broadcast_to(coef0[k], (8, LANES))
    sum_done(1)


def finish(ps_late, e, v, fac, wgt, coef, out_ps, out_carry, ps, carry, sems):
    rx, ry, rz = ps.shape
    nz = rz // LANES
    late = pltpu.make_async_copy(ps_late, out_ps.at[1], sems.at[0])
    late.start()
    part = max(1, rx // WRITES)
    c = [coef[k] for k in range(ITERS)]
    copies = [late]
    for q, low in enumerate(range(0, rx, part)):
        size = min(part, rx - low)

        def plane(x, _):
            for z in range(nz):
                lanes = slice(z * LANES, (z + 1) * LANES)
                for r in range(0, ry, 8):
                    rows = slice(HY + r, HY + r + 8)
                    a = c[0] * e[x + HX, z, rows]
                    for k in range(1, ITERS):
                        a = a + c[k] * v[k - 1, x + HX, z, rows]
                    ps[x, r:r + 8, lanes] = wgt[0, x, r:r + 8, lanes] * a
                    carry[x, r:r + 8, lanes] = fac[0, x, r:r + 8, lanes] * a
            return 0

        sweep(low, low + size, LAST, plane)
        piece = pl.ds(low, size)
        copies.append(pltpu.make_async_copy(ps.at[piece], out_ps.at[0, piece], sems.at[1 + 2 * q]))
        copies.append(pltpu.make_async_copy(carry.at[piece], out_carry.at[piece], sems.at[2 + 2 * q]))
        copies[-2].start()
        copies[-1].start()
    for copy in copies:
        copy.wait()


def per_device(n, m, temp_before, temp_after, melt_phase, objective_grad, laser_path):
    steps, rx, ry, rz = temp_before.shape
    ex, ey = rx + 2 * HX, ry + 2 * HY
    nz = rz // LANES
    waves = (max(n, m) - 2).bit_length()
    f32 = jnp.float32
    vm = pl.BlockSpec(memory_space=pltpu.VMEM)
    dma = pltpu.SemaphoreType.DMA
    results = pl.pallas_call(
        functools.partial(kernel, n, m),
        out_shape=tuple(
            pltpu.VMEM(shape, f32)
            for shape in (
                (rx, ry, rz),
                (ex, nz, ey, LANES),
                (ITERS - 1, ex, nz, ey, LANES),
                (steps, rx, ry, rz),
                (steps, rx, ry, rz),
                (ITERS, 8, LANES),
            )
        ),
        in_specs=[pl.BlockSpec(memory_space=pl.ANY)] * 4 + [pl.BlockSpec(memory_space=pltpu.SMEM)],
        out_specs=(vm,) * 6,
        scratch_shapes=[
            pltpu.VMEM((2, rx, ry, rz), f32),
            pltpu.VMEM((2, rx, ry, rz), f32),
            pltpu.VMEM((2, rx, ry, rz), jnp.int32),
            pltpu.VMEM((2, ex, nz, ey, LANES), f32),
            pltpu.VMEM((ex, nz, ey, LANES), f32),
            pltpu.VMEM((rx, nz, ry, LANES), f32),
            pltpu.VMEM((rx, nz, ry, LANES), f32),
            pltpu.VMEM((2, 8, LANES), f32),
            pltpu.VMEM((2, n * m, LANES), f32),
            dma((8 + 2 * nz,)),
            dma((4, 8)), dma((4, 8)),
            dma((4,)), dma((4,)),
            dma((2,)), dma((2,)),
            pltpu.SemaphoreType.REGULAR((waves,)),
        ],
        compiler_params=pltpu.CompilerParams(
            collective_id=0, has_side_effects=True, vmem_limit_bytes=56 * 1024 * 1024
        ),
    )(temp_before, temp_after, melt_phase, objective_grad, laser_path)
    hbm = pl.BlockSpec(memory_space=pl.ANY)
    parts = -(-rx // max(1, rx // WRITES))
    return pl.pallas_call(
        finish,
        out_shape=(
            jax.ShapeDtypeStruct((steps, rx, ry, rz), f32),
            jax.ShapeDtypeStruct((rx, ry, rz), f32),
        ),
        in_specs=[vm] * 6,
        out_specs=(hbm, hbm),
        scratch_shapes=[pltpu.VMEM((rx, ry, rz), f32), pltpu.VMEM((rx, ry, rz), f32), dma((1 + 2 * parts,))],
        compiler_params=pltpu.CompilerParams(vmem_limit_bytes=4 * 1024 * 1024),
    )(*results)


def solution(mesh):
    spec = P(None, "scan", "track", None)
    return jax.shard_map(
        functools.partial(per_device, mesh.shape["scan"], mesh.shape["track"]),
        mesh=mesh,
        in_specs=(spec, spec, spec, spec, P()),
        out_specs=(spec, P("scan", "track", None)),
        check_vma=False,
    )
```

```python
import functools

import jax
import jax.numpy as jnp
from jax import lax
from jax.experimental import pallas as pl
from jax.experimental.pallas import tpu as pltpu
from jax.sharding import PartitionSpec as P

ITERS = 4
CAPS = (0.6, 2.0, 0.9)
ABSORBS = (0.35, 0.5, 0.65)
spot_radius = 3.0
decay_depth = 4.0
spot_peak = 4.0

SHIFT = 7.25
SCALE = 3.0

HX = 4
HY = 8

DIRS = ((-1, 0), (1, 0), (-1, -1), (-1, 1), (1, -1), (1, 1), (0, -1), (0, 1))
BACK = ((-1, 0),)
AHEAD = ((1, -1), (1, 0), (1, 1))
ASIDE = ((0, -1), (0, 1))
PAIRS = tuple((i, j) for i in range(ITERS) for j in range(i, ITERS)) + ((ITERS - 1, ITERS),)
MESH = pl.DeviceIdType.MESH
LANES = 128
DIAG, CARRY, RHS, LAST = 4, 16, 16, 4
TRIPS = 2
DOT_TRIPS = 2
WRITES = 4


def lookup(melt, values):
    return jnp.where(
        melt == 0,
        jnp.float32(values[0]),
        jnp.where(melt == 1, jnp.float32(values[1]), jnp.float32(values[2])),
    )


def solve_small(g):
    def gram(i, j):
        return g[(min(i, j), max(i, j))]

    n = ITERS
    h = {}
    for i in range(n):
        for j in range(i, n):
            value = SCALE * gram(i + 1, j) + SHIFT * gram(i, j)
            if i > 0:
                value = value + SCALE * gram(i - 1, j)
            h[(i, j)] = value
    low, inv, y = {}, {}, {}
    for j in range(n):
        d = h[(j, j)]
        for k in range(j):
            d = d - low[(j, k)] * low[(j, k)] * inv[("d", k)]
        good = d > 1e-7 * h[(j, j)]
        inv[("d", j)] = jnp.where(good, d, 0.0)
        inv[j] = jnp.where(good, 1.0 / jnp.where(good, d, 1.0), 0.0)
        for i in range(j + 1, n):
            t = h[(j, i)]
            for k in range(j):
                t = t - low[(i, k)] * low[(j, k)] * inv[("d", k)]
            low[(i, j)] = t * inv[j]
    for i in range(n):
        t = gram(0, i)
        for k in range(i):
            t = t - low[(i, k)] * y[k]
        y[i] = t
    a = [None] * n
    for i in reversed(range(n)):
        t = y[i] * inv[i]
        for k in range(i + 1, n):
            t = t - low[(k, i)] * a[k]
        a[i] = t
    return a


def sweep(start, stop, group, body):
    trips = (stop - start) // group
    if trips > 1:
        def trip(p, _):
            for g in range(group):
                body(start + p * group + g, 0)
            return 0

        lax.fori_loop(0, trips, trip, 0)
        start += trips * group
    for x in range(start, stop):
        body(x, 0)


def kernel(n, m, tb_in, ta_in, melt_in, grad_in, path, ps_late, er0, v, fac, wgt, weights_out,
           tb, ta, melt, e1, ec0, cs, cr, part, red,
           load_sem, h_send, h_recv, c_send, c_recv, r_send, r_recv, known):
    rx, ry, rz = tb.shape[1:]
    ex, ey = rx + 2 * HX, ry + 2 * HY
    nz = rz // LANES
    d = lax.axis_index("scan")
    t = lax.axis_index("track")

    def exists(dx, dy):
        ok = None
        if dx < 0:
            ok = d > 0
        if dx > 0:
            ok = d < n - 1
        if dy != 0:
            oky = (t > 0) if dy < 0 else (t < m - 1)
            ok = oky if ok is None else jnp.logical_and(ok, oky)
        return ok

    def at_distance(r):
        for dx, dy in DIRS:
            ok = None
            if dx != 0:
                ok = (d >= r) if dx < 0 else (d < n - r)
            if dy != 0:
                oky = (t >= r) if dy < 0 else (t < m - r)
                ok = oky if ok is None else jnp.logical_and(ok, oky)
            if (dx == 0 or r < n) and (dy == 0 or r < m):
                yield ok, (d + dx * r, t + dy * r)

    def greet(sem, r):
        for ok, device in at_distance(r):
            @pl.when(ok)
            def _(device=device):
                pl.semaphore_signal(sem, inc=1, device_id=device, device_id_type=MESH)

    def greeted(sem, r):
        count = jnp.int32(0)
        for ok, _ in at_distance(r):
            count = count + ok.astype(jnp.int32)
        pl.semaphore_wait(sem, count)

    barrier = pltpu.get_barrier_semaphore()
    greet(barrier, 1)

    def zero_halo(ref):
        @pl.when(d == 0)
        def _():
            ref[0:HX] = jnp.zeros((HX, nz, ey, LANES), jnp.float32)

        @pl.when(d == n - 1)
        def _():
            ref[ex - HX:ex] = jnp.zeros((HX, nz, ey, LANES), jnp.float32)

        @pl.when(t == 0)
        def _():
            ref[:, :, 0:HY] = jnp.zeros((ex, nz, HY, LANES), jnp.float32)

        @pl.when(t == m - 1)
        def _():
            ref[:, :, ey - HY:ey] = jnp.zeros((ex, nz, HY, LANES), jnp.float32)

    def zs(z):
        return slice(z * LANES, (z + 1) * LANES)

    loads = []
    for q, (s, kind) in enumerate([(1, 2), (1, 0), (1, 1), (1, 3), (0, 0), (0, 1), (0, 2), (0, 3)]):
        if kind == 2:
            where = e1.at[0] if s == 1 else er0
            parts = [
                pltpu.make_async_copy(
                    grad_in.at[s, :, :, pl.ds(z * LANES, LANES)],
                    where.at[pl.ds(HX, rx), z, pl.ds(HY, ry)],
                    load_sem.at[8 + s * nz + z],
                )
                for z in range(nz)
            ]
        else:
            src, dst = ((tb_in, tb), (melt_in, melt), None, (ta_in, ta))[kind]
            parts = [pltpu.make_async_copy(src.at[s], dst.at[s], load_sem.at[q])]
        loads.append(parts)

    def loaded(*which):
        for q in which:
            for c in loads[q]:
                c.wait()

    for c in loads[0]:
        c.start()
    zero_halo(e1.at[0])
    zero_halo(er0)

    def terms(s, x):
        base = lookup(melt[s, x], CAPS)
        h = jnp.tanh(tb[s, x])
        return base * (1.0 + 0.5 * h), base, h

    def diagonals(s, cap_ref):
        def body(x, _):
            cap, _, _ = terms(s, x)
            cap = (cap + (6.0 - SHIFT)) * (1.0 / SCALE)
            for z in range(nz):
                cap_ref[x + HX, z, HY:HY + ry] = cap[:, zs(z)]
            return 0

        sweep(0, rx, DIAG, body)

    def factors(s):
        def body(x, _):
            cap, base, h = terms(s, x)
            slope = base * 0.5 * (1.0 - h * h)
            fac[s, x] = cap - slope * (ta[s, x] - tb[s, x])
            return 0

        lax.fori_loop(0, rx, body, 0)

    waves = known.shape[0]

    def spread(step):
        if 0 < step <= waves:
            greeted(known.at[step - 1], 2 ** (step - 1))
        if step < waves:
            greet(known.at[step], 2 ** step)
        return step + 1

    loaded(0)
    for parts in loads[1:]:
        for c in parts:
            c.start()
    greeted(barrier, 1)

    def span(delta, low, count, width):
        if delta == 0:
            return low, low, count
        if delta > 0:
            return low + count - width, low - width, width
        return low, low + count, width

    def halo_copy(ref, which, q):
        dx, dy = DIRS[q]
        wide = ITERS if which in (0, 2) else ITERS - 1
        if dx != 0 and dy != 0:
            wx = wy = wide - 2 if dx > 0 and dy > 0 else wide - 1
        else:
            wx = wide - 1 if dx > 0 else wide
            wy = wide - 1 if dy > 0 else wide
        x_src, x_dst, x_size = span(dx, HX, rx, wx)
        y_src, y_dst, y_size = span(dy, HY, ry, wy)
        if which == 2 and dx == 0:
            x_size = rx + ITERS - 1
        return pltpu.make_async_remote_copy(
            src_ref=ref.at[pl.ds(x_src, x_size), slice(None), pl.ds(y_src, y_size)],
            dst_ref=ref.at[pl.ds(x_dst, x_size), slice(None), pl.ds(y_dst, y_size)],
            send_sem=h_send.at[which, q],
            recv_sem=h_recv.at[which, q],
            device_id=(d + dx, t + dy),
            device_id_type=MESH,
        )

    def halo_start(ref, which, wanted=DIRS):
        for q, (dx, dy) in enumerate(DIRS):
            if (dx, dy) in wanted:
                @pl.when(exists(dx, dy))
                def _(q=q):
                    halo_copy(ref, which, q).start()

    def halo_wait(ref, which, wanted=DIRS):
        for q, (dx, dy) in enumerate(DIRS):
            if (dx, dy) in wanted:
                @pl.when(exists(-dx, -dy))
                def _(q=q):
                    halo_copy(ref, which, q).wait_recv()

    def halo_done(ref, which, wanted=DIRS):
        for q, (dx, dy) in enumerate(DIRS):
            if (dx, dy) in wanted:
                @pl.when(exists(dx, dy))
                def _(q=q):
                    halo_copy(ref, which, q).wait_send()

    lane8 = lax.broadcasted_iota(jnp.int32, (8, LANES), 1)
    first, final = lane8 == 0, lane8 == LANES - 1

    def advance(v0, cap_ref, k, start, count, tiles):
        at = [v0] + [v.at[q] for q in range(ITERS - 1)]
        trips = TRIPS if count % TRIPS == 0 and count * len(tiles) > 36 else 1
        planes = count // trips

        def trip(p, _):
            x = start + planes * p
            for r in tiles:
                c = [[at[k][x + q, z, r:r + 8] for z in range(nz)] for q in range(-1, planes + 1)]
                for q in range(planes):
                    mid = c[q + 1]
                    up = [pltpu.roll(w, 1, 1) for w in mid]
                    down = [pltpu.roll(w, LANES - 1, 1) for w in mid]
                    for z in range(nz):
                        above = jnp.where(first, up[z - 1] if z > 0 else 0.0, up[z])
                        below = jnp.where(final, down[z + 1] if z < nz - 1 else 0.0, down[z])
                        beside = (c[q][z] + c[q + 2][z]) + (above + below)
                        beside = beside + (at[k][x + q, z, r - 1:r + 7] + at[k][x + q, z, r + 1:r + 9])
                        new = cap_ref[x + q, z, r:r + 8] * mid[z] - beside * (1.0 / SCALE)
                        if k > 0:
                            new = new - at[k - 1][x + q, z, r:r + 8]
                        at[k + 1][x + q, z, r:r + 8] = new
            return 0

        if trips == 1:
            trip(0, 0)
        else:
            lax.fori_loop(0, trips, trip, 0)

    def inner_part(k):
        low, high = HY + 4 + k, HY + ry - 4 - k
        return low, high, [min(r, high - 8) for r in range(low, high, 8)]

    def powers_inside(v0, cap_ref):
        for k in range(ITERS - 1):
            advance(v0, cap_ref, k, HX + 1 + k, rx - 2 - 2 * k, inner_part(k)[2])

    def powers_around(v0, cap_ref):
        for k in range(ITERS - 1):
            low, high, tiles = inner_part(k)
            edge = [low - 8, high]
            first_plane = HX - (ITERS - 2) + k
            advance(v0, cap_ref, k, first_plane, HX + 1 + k - first_plane, edge[:1] + tiles + edge[1:])
            advance(v0, cap_ref, k, HX + rx - 1 - k, ITERS, edge[:1] + tiles + edge[1:])
            advance(v0, cap_ref, k, HX + 1 + k, rx - 2 - 2 * k, edge)
            zero_halo(v.at[k])

    def dots(v0, cap_ref, slot):
        at = [v0] + [v.at[k] for k in range(ITERS - 1)]
        group = max(1, rx // DOT_TRIPS)

        def body(p, acc):
            acc = list(acc)
            for g in range(group):
                x = HX + p * group + g
                for r in range(HY, HY + ry, 8):
                    tips = [at[-1][x, z, r:r + 8] for z in range(nz)]
                    for z in range(nz):
                        vals = [ref[x, z, r:r + 8] for ref in at[:-1]] + [tips[z]]
                        over = tips[z + 1] if z < nz - 1 else 0.0
                        below = pltpu.roll(jnp.where(first, over, tips[z]), LANES - 1, 1)
                        after = at[-1][x + 1, z, r:r + 8] + at[-1][x, z, r + 1:r + 9] + below
                        vals.append(cap_ref[x, z, r:r + 8] * tips[z] - after * (2.0 / SCALE))
                        for q, (i, j) in enumerate(PAIRS):
                            acc[q] = acc[q] + vals[i] * vals[j]
            return tuple(acc)

        acc = lax.fori_loop(0, rx // group, body, tuple(jnp.zeros((8, LANES), jnp.float32) for _ in PAIRS))
        lane = lax.broadcasted_iota(jnp.int32, (1, LANES), 1)
        row = jnp.zeros((1, LANES), jnp.float32)
        for q, a in enumerate(acc):
            s = jnp.sum(jnp.sum(a, axis=0, keepdims=True), axis=1, keepdims=True)
            row = jnp.where(lane == q, s, row)
        part[slot, 0:1] = row

    me = d * m + t
    others = n * m - 1

    def sum_copy(slot, device):
        return pltpu.make_async_remote_copy(
            src_ref=part.at[slot, pl.ds(0, 1)],
            dst_ref=red.at[slot, pl.ds(me, 1)],
            send_sem=r_send.at[slot],
            recv_sem=r_recv.at[slot],
            device_id=device,
            device_id_type=MESH,
        )

    def sum_start(slot):
        for j in range(m):
            row = jnp.where(2 * t < m, m - 1 - j, j)
            for k in range(n):
                column = lax.rem(d + (n // 2 + k) % n, n)
                if (n // 2 + k) % n == 0:
                    @pl.when(row != t)
                    def _(row=row):
                        sum_copy(slot, (d, row)).start()
                else:
                    sum_copy(slot, (column, row)).start()
        red[slot, pl.ds(me, 1)] = part[slot, 0:1]

    def all_others(ref, sem):
        view = ref.at[pl.ds(0, others)]
        pltpu.make_async_copy(view, view, sem).wait()

    def sum_end(slot):
        all_others(red.at[slot], r_recv.at[slot])
        total = jnp.sum(red[slot], axis=0, keepdims=True)
        lane = lax.broadcasted_iota(jnp.int32, (1, LANES), 1)
        g = {}
        for q, pair in enumerate(PAIRS):
            g[pair] = jnp.sum(jnp.where(lane == q, total, 0.0), axis=1, keepdims=True)
        g[PAIRS[-1]] = g[PAIRS[-1]] - g[(ITERS - 2, ITERS - 1)]
        return solve_small(g)

    def sum_done(slot):
        all_others(red.at[slot], r_send.at[slot])

    def adjoint(v0, coef, x, z, r=0, size=None):
        rows = slice(HY + r, HY + r + (size or ry))
        out = coef[0] * v0[x + HX, z, rows]
        for k in range(1, ITERS):
            out = out + coef[k] * v[k - 1, x + HX, z, rows]
        return out

    def weights(s):
        width = m * ry
        yy = (t * ry + lax.broadcasted_iota(jnp.int32, (ry, 128), 0)).astype(jnp.float32)
        xx = (d * rx + lax.broadcasted_iota(jnp.int32, (ry, 128), 1)).astype(jnp.float32)
        two = 2.0 * spot_radius * spot_radius
        surface = jnp.zeros((ry, 128), jnp.float32)
        for k in range(path.shape[1]):
            cell = path[s, k]
            dx = xx - lax.div(cell, jnp.int32(width)).astype(jnp.float32)
            dy = yy - lax.rem(cell, jnp.int32(width)).astype(jnp.float32)
            surface = surface + jnp.exp(-dx * dx / two) * jnp.exp(-dy * dy / two)
        zz = lax.broadcasted_iota(jnp.int32, (1, rz), 1).astype(jnp.float32)
        fall = spot_peak * jnp.exp(-zz / decay_depth)
        lane = lax.broadcasted_iota(jnp.int32, (ry, 128), 1)

        def body(x, _):
            column = jnp.sum(jnp.where(lane == x, surface, 0.0), axis=1, keepdims=True)
            wgt[s, x] = lookup(melt[s, x], ABSORBS) * (1.0 + column * fall)
            return 0

        lax.fori_loop(0, rx, body, 0)

    halo_start(e1.at[0], 0)
    step = spread(0)
    loaded(1, 2)
    diagonals(1, e1.at[1])
    halo_start(e1.at[1], 3)
    step = spread(step)
    loaded(4, 5)
    diagonals(0, ec0)
    step = spread(step)
    loaded(3)
    factors(1)
    loaded(7)
    factors(0)
    while step < waves:
        step = spread(step)
    spread(step)
    powers_inside(e1.at[0], e1.at[1])
    halo_wait(e1.at[0], 0)
    halo_wait(e1.at[1], 3)
    powers_around(e1.at[0], e1.at[1])
    dots(e1.at[0], e1.at[1], 0)
    sum_start(0)
    loaded(6)
    halo_start(er0, 2, BACK)
    halo_start(ec0, 1)
    weights(1)
    weights(0)
    coef = sum_end(0)

    tail = ITERS - 1
    body = rx - tail
    PIECES = ((body, tail, 0, ry), (0, body, 0, ITERS), (0, body, ry - tail, tail), (0, body, ITERS, ry - tail - ITERS))

    def carry_copy(c):
        x, xs, y, ys = PIECES[c]
        piece = (pl.ds(x, xs), slice(None), pl.ds(y, ys))
        return pltpu.make_async_remote_copy(
            src_ref=cs.at[piece], dst_ref=cr.at[piece], send_sem=c_send.at[c], recv_sem=c_recv.at[c],
            device_id=(d + 1, t), device_id_type=MESH)

    def carry_start(*which):
        @pl.when(d < n - 1)
        def _():
            for c in which:
                carry_copy(c).start()

    def carry_make(start, stop, rows):
        def plane(x, _):
            for z in range(nz):
                for r, size in rows:
                    cs[x, z, r:r + size] = fac[1, x, r:r + size, zs(z)] * adjoint(e1.at[0], coef, x, z, r, size)
            return 0

        sweep(start, stop, CARRY, plane)

    def rhs_make(*which):
        @pl.when(d > 0)
        def _():
            for c in which:
                carry_copy(c).wait_recv()
            start, count = PIECES[which[0]][:2]

            def plane(x, _):
                for c in which:
                    _, _, y, ys = PIECES[c]
                    for z in range(nz):
                        here = (x + HX, z, slice(HY + y, HY + y + ys))
                        er0[here] = er0[here] + cr[x, z, y:y + ys]
                return 0

            sweep(start, start + count, RHS, plane)

    carry_make(body, rx, ((0, ry),))
    carry_start(0)
    carry_make(0, body, ((0, 8), (ry - 8, 8)))
    carry_start(1, 2)
    carry_make(0, body, ((8, ry - 16),))
    carry_start(3)
    rhs_make(0)
    halo_start(er0, 2, AHEAD)
    halo_done(er0, 2, BACK)
    halo_wait(er0, 2, BACK)

    @pl.when(d < n - 1)
    def _():
        for x in range(ITERS):
            for z in range(nz):
                here = (HX + rx + x, z, slice(HY, HY + ry))
                er0[here] = er0[here] + cs[x, z]

    rhs_make(1, 2)
    halo_start(er0, 2, ASIDE)

    def late(x, _):
        for z in range(nz):
            ps_late[x, :, zs(z)] = wgt[1, x, :, zs(z)] * adjoint(e1.at[0], coef, x, z)
        return 0

    lax.fori_loop(0, rx, late, 0)
    rhs_make(3)
    powers_inside(er0, ec0)
    halo_wait(ec0, 1)
    halo_wait(er0, 2, AHEAD + ASIDE)
    powers_around(er0, ec0)
    dots(er0, ec0, 1)
    sum_start(1)
    halo_done(e1.at[0], 0)
    halo_done(e1.at[1], 3)
    halo_done(ec0, 1)
    halo_done(er0, 2, AHEAD + ASIDE)
    sum_done(0)

    @pl.when(d < n - 1)
    def _():
        for c in range(len(PIECES)):
            carry_copy(c).wait_send()

    coef0 = sum_end(1)
    for k in range(ITERS):
        weights_out[k] = jnp.broadcast_to(coef0[k], (8, LANES))
    sum_done(1)


def finish(ps_late, e, v, fac, wgt, coef, out_ps, out_carry, ps, carry, sems):
    rx, ry, rz = ps.shape
    nz = rz // LANES
    late = pltpu.make_async_copy(ps_late, out_ps.at[1], sems.at[0])
    late.start()
    part = max(1, rx // WRITES)
    c = [coef[k] for k in range(ITERS)]
    copies = [late]
    for q, low in enumerate(range(0, rx, part)):
        size = min(part, rx - low)

        def plane(x, _):
            for z in range(nz):
                lanes = slice(z * LANES, (z + 1) * LANES)
                for r in range(0, ry, 8):
                    rows = slice(HY + r, HY + r + 8)
                    a = c[0] * e[x + HX, z, rows]
                    for k in range(1, ITERS):
                        a = a + c[k] * v[k - 1, x + HX, z, rows]
                    ps[x, r:r + 8, lanes] = wgt[0, x, r:r + 8, lanes] * a
                    carry[x, r:r + 8, lanes] = fac[0, x, r:r + 8, lanes] * a
            return 0

        sweep(low, low + size, LAST, plane)
        piece = pl.ds(low, size)
        copies.append(pltpu.make_async_copy(ps.at[piece], out_ps.at[0, piece], sems.at[1 + 2 * q]))
        copies.append(pltpu.make_async_copy(carry.at[piece], out_carry.at[piece], sems.at[2 + 2 * q]))
        copies[-2].start()
        copies[-1].start()
    for copy in copies:
        copy.wait()


def per_device(n, m, temp_before, temp_after, melt_phase, objective_grad, laser_path):
    steps, rx, ry, rz = temp_before.shape
    ex, ey = rx + 2 * HX, ry + 2 * HY
    nz = rz // LANES
    waves = (max(n, m) - 2).bit_length()
    f32 = jnp.float32
    vm = pl.BlockSpec(memory_space=pltpu.VMEM)
    dma = pltpu.SemaphoreType.DMA
    results = pl.pallas_call(
        functools.partial(kernel, n, m),
        out_shape=tuple(
            pltpu.VMEM(shape, f32)
            for shape in (
                (rx, ry, rz),
                (ex, nz, ey, LANES),
                (ITERS - 1, ex, nz, ey, LANES),
                (steps, rx, ry, rz),
                (steps, rx, ry, rz),
                (ITERS, 8, LANES),
            )
        ),
        in_specs=[pl.BlockSpec(memory_space=pl.ANY)] * 4 + [pl.BlockSpec(memory_space=pltpu.SMEM)],
        out_specs=(vm,) * 6,
        scratch_shapes=[
            pltpu.VMEM((2, rx, ry, rz), f32),
            pltpu.VMEM((2, rx, ry, rz), f32),
            pltpu.VMEM((2, rx, ry, rz), jnp.int32),
            pltpu.VMEM((2, ex, nz, ey, LANES), f32),
            pltpu.VMEM((ex, nz, ey, LANES), f32),
            pltpu.VMEM((rx, nz, ry, LANES), f32),
            pltpu.VMEM((rx, nz, ry, LANES), f32),
            pltpu.VMEM((2, 8, LANES), f32),
            pltpu.VMEM((2, n * m, LANES), f32),
            dma((8 + 2 * nz,)),
            dma((4, 8)), dma((4, 8)),
            dma((4,)), dma((4,)),
            dma((2,)), dma((2,)),
            pltpu.SemaphoreType.REGULAR((waves,)),
        ],
        compiler_params=pltpu.CompilerParams(
            collective_id=0, has_side_effects=True, vmem_limit_bytes=56 * 1024 * 1024
        ),
    )(temp_before, temp_after, melt_phase, objective_grad, laser_path)
    hbm = pl.BlockSpec(memory_space=pl.ANY)
    parts = -(-rx // max(1, rx // WRITES))
    return pl.pallas_call(
        finish,
        out_shape=(
            jax.ShapeDtypeStruct((steps, rx, ry, rz), f32),
            jax.ShapeDtypeStruct((rx, ry, rz), f32),
        ),
        in_specs=[vm] * 6,
        out_specs=(hbm, hbm),
        scratch_shapes=[pltpu.VMEM((rx, ry, rz), f32), pltpu.VMEM((rx, ry, rz), f32), dma((1 + 2 * parts,))],
        compiler_params=pltpu.CompilerParams(vmem_limit_bytes=4 * 1024 * 1024),
    )(*results)


def solution(mesh):
    spec = P(None, "scan", "track", None)
    return jax.shard_map(
        functools.partial(per_device, mesh.shape["scan"], mesh.shape["track"]),
        mesh=mesh,
        in_specs=(spec, spec, spec, spec, P()),
        out_specs=(spec, P("scan", "track", None)),
        check_vma=False,
    )
```
